32 devices in a mesh: real: 4 (over z), rows: 4 (over y, core), field: 2 (over x).
Axes of the slice: x: 2, y: 2, z: 4, core: 2. Of those that a mesh axis runs over, the one named last changes fastest.
Arguments:
- sims: bfloat16 [4, 2, 2048, 2048], P('real', 'field', 'rows'), may hold values from -6 to 6
- data: bfloat16 [2, 2048, 2048], P('field', 'rows'), may hold values from -6 to 6
- mask_flags: int32 [16, 16], P('rows'), may hold values 0 or 1
- bins: int32 [512, 512], P(None, 'rows'), may hold values from 0 to 63
- cl_signal: float32 [2, 64], P('field'), may hold values from 0.5 to 4
- cl_noise: float32 [2, 64], P('field'), may hold values from 0.1 to 2
- norm: float32 [64], replicated, may hold values from 0.5 to 2
- matching: int32 [4], replicated, may hold values from 0 to 3, each once
Outputs:
- estimates: float32 [4, 2, 2, 512, 512], P('real', None, None, None, 'rows')
The draws below stay inside these ranges and needn't reach their ends.
Inputs may be any that keep to these rules, and one draw needn't show every extreme that they name: `matching`: each realization index appears exactly once.
All inputs are finite; a program needn't handle non-finite values. No bound on the sum of `mask_flags` on one device may be relied on, other than what follows from the above.
Results may differ from the reference program's by a relative error of at most 0.011.
Values may be sent and summed in bfloat16 or wider, within the bound.
A program may use at most 128 MiB of HBM per device.

```python
import math
import jax
import jax.numpy as jnp
from jax import lax

NPIX = 2048
KF = 512
NB = 64
TILE = 128
FIELDS = 2
REALS = 4


def with_ends(entries, stream_key, least, high):
    longest = entries.shape.index(max(entries.shape))
    spots = []
    for shift in (0, 1):
        where = [jax.random.randint(jax.random.fold_in(stream_key, axis), (), 0, length) for axis, length in enumerate(entries.shape)]
        where[longest] = (where[longest] + shift) % entries.shape[longest]
        spots.append(tuple(where))
    return entries.at[spots[0]].set(least).at[spots[1]].set(high)


def block_scale(key, extent, cuts, least, high):
    level, own = 1.0, jax.random.fold_in(key, 6)
    for dim, shards_of in cuts:
        draws = jnp.exp(jax.random.uniform(jax.random.fold_in(own, dim), (shards_of,), jnp.float32, least / len(cuts), high / len(cuts)))
        level = level * jnp.repeat(draws, extent[dim] // shards_of).reshape([-1 if axis == dim else 1 for axis in range(len(extent))])
    return level


def noise(stream_key, extent, scale, bound, pieces=(), kind=jnp.bfloat16):
    factor_of = block_scale(stream_key, extent, pieces, -0.22, 0.18) if pieces else 1.0
    values = jax.random.normal(stream_key, extent, jnp.float32) * scale * factor_of
    return jnp.minimum(jnp.maximum(values, -bound), bound).astype(kind)


def setup_inputs(seed: int = 0) -> dict:
    arg_keys = jax.random.split(jax.random.key(seed), 9)
    sims = noise(arg_keys[0], (REALS, FIELDS, NPIX, NPIX), 1.0, 6.0, ((0, 4), (1, 2), (2, 4)))
    data = noise(arg_keys[1], (FIELDS, NPIX, NPIX), 1.0, 6.0, ((0, 2), (1, 4)))
    mask_flags = with_ends((jax.random.randint(arg_keys[2], (NPIX // TILE, NPIX // TILE), 0, 8) < 7).astype(jnp.int32), jax.random.fold_in(arg_keys[2], 1), 0, 1)
    bins = with_ends(jax.random.randint(arg_keys[3], (KF, KF), 0, NB), jax.random.fold_in(arg_keys[3], 1), 0, NB - 1).astype(jnp.int32)
    cl_signal = jnp.clip(jnp.exp(math.log(4.0) - 2.0794415 * jax.random.uniform(arg_keys[4], (FIELDS, NB), jnp.float32) ** block_scale(arg_keys[4], (FIELDS, NB), ((0, 2),), -0.2, 0.2)), 0.5, 4.0)
    cl_noise = jnp.clip(jnp.exp(math.log(2.0) - 2.9957323 * jax.random.uniform(arg_keys[5], (FIELDS, NB), jnp.float32) ** block_scale(arg_keys[5], (FIELDS, NB), ((0, 2),), -0.2, 0.2)), 0.1, 2.0)
    norm = jnp.clip(jnp.exp(jax.random.uniform(arg_keys[6], (NB,), jnp.float32, math.log(0.5), math.log(2.0))), 0.5, 2.0)
    matching = jax.random.permutation(arg_keys[7], REALS).astype(jnp.int32)
    return {"sims": sims, "data": data, "mask_flags": mask_flags, "bins": bins, "cl_signal": cl_signal, "cl_noise": cl_noise, "norm": norm, "matching": matching}


HIGH = lax.Precision.HIGHEST


def tables(npix, kf, scale):
    pixel = jnp.arange(npix, dtype=jnp.int32)
    freq = jnp.arange(kf, dtype=jnp.int32) - kf // 2
    phase = jnp.mod(pixel[:, None] * freq[None, :], npix)
    angle = phase.astype(jnp.float32) * (2.0 * math.pi / npix)
    return (jnp.cos(angle) * scale).astype(jnp.bfloat16), (jnp.sin(angle) * scale).astype(jnp.bfloat16)


def expand_mask(flags, tile):
    first, second = flags.shape
    full = jnp.broadcast_to(flags[:, None, :, None], (first, tile, second, tile))
    return full.reshape(first * tile, second * tile) > 0


def column_part(maps, cos_t, sin_t):
    count, height, width = maps.shape
    flat = maps.reshape(count * height, width)
    a_re = jnp.dot(flat, cos_t, preferred_element_type=jnp.float32).astype(jnp.bfloat16).reshape(count, height, -1)
    a_im = (-jnp.dot(flat, sin_t, preferred_element_type=jnp.float32)).astype(jnp.bfloat16).reshape(count, height, -1)
    return a_re, a_im


def row_part(a_re, a_im, cos_t, sin_t):
    cos_w = cos_t.astype(jnp.float32)
    sin_w = sin_t.astype(jnp.float32)
    are = a_re.astype(jnp.float32)
    aim = a_im.astype(jnp.float32)
    x_re = jnp.einsum('yk,myj->mkj', cos_w, are, precision=HIGH) + jnp.einsum('yk,myj->mkj', sin_w, aim, precision=HIGH)
    x_im = jnp.einsum('yk,myj->mkj', cos_w, aim, precision=HIGH) - jnp.einsum('yk,myj->mkj', sin_w, are, precision=HIGH)
    return x_re, x_im


def forward(maps, cos_t, sin_t):
    a_re, a_im = column_part(maps, cos_t, sin_t)
    return row_part(a_re, a_im, cos_t, sin_t)


def inverse(z_re, z_im, icos, isin):
    count = z_re.shape[0]
    icw = icos.astype(jnp.float32)
    isw = isin.astype(jnp.float32)
    zr = z_re.astype(jnp.float32)
    zi = z_im.astype(jnp.float32)
    y_re = (jnp.einsum('yk,mkj->myj', icw, zr, precision=HIGH) - jnp.einsum('yk,mkj->myj', isw, zi, precision=HIGH)).astype(jnp.bfloat16)
    y_im = (jnp.einsum('yk,mkj->myj', icw, zi, precision=HIGH) + jnp.einsum('yk,mkj->myj', isw, zr, precision=HIGH)).astype(jnp.bfloat16)
    height = y_re.shape[1]
    flat_re = y_re.reshape(count * height, -1)
    flat_im = y_im.reshape(count * height, -1)
    out = jnp.dot(flat_re, icos.T, preferred_element_type=jnp.float32) - jnp.dot(flat_im, isin.T, preferred_element_type=jnp.float32)
    return out.astype(jnp.bfloat16).reshape(count, height, -1)


def filter_legs(x_re, x_im, wcell, gcell, lx, ly):
    grad_x = lx * gcell
    grad_y = ly * gcell
    z_re = jnp.stack([wcell * x_re, -grad_x * x_im, -grad_y * x_im])
    z_im = jnp.stack([wcell * x_im, grad_x * x_re, grad_y * x_re])
    return z_re.astype(jnp.bfloat16), z_im.astype(jnp.bfloat16)


def reference(sims, data, mask_flags, bins, cl_signal, cl_noise, norm, matching):
    mask = expand_mask(mask_flags, TILE)
    cos_t, sin_t = tables(NPIX, KF, NPIX ** -0.5)
    icos, isin = tables(NPIX, KF, KF ** -0.5)
    freq = (jnp.arange(KF, dtype=jnp.int32) - KF // 2).astype(jnp.float32) * (2.0 * math.pi / NPIX)
    lx = jnp.broadcast_to(freq[None, :], (KF, KF))
    ly = jnp.broadcast_to(freq[:, None], (KF, KF))
    weight_vals = 1.0 / (cl_signal + cl_noise)
    grad_vals = cl_signal * weight_vals
    wcell = weight_vals[:, bins]
    gcell = grad_vals[:, bins]
    ncell = norm[bins]

    def legs_of(maps):
        masked = jnp.where(mask[None], maps, jnp.zeros_like(maps))
        x_re, x_im = forward(masked, cos_t, sin_t)
        parts = [filter_legs(x_re[f], x_im[f], wcell[f], gcell[f], lx, ly) for f in range(FIELDS)]
        z_re = jnp.concatenate([p[0] for p in parts], axis=0)
        z_im = jnp.concatenate([p[1] for p in parts], axis=0)
        return inverse(z_re, z_im, icos, isin).reshape(FIELDS, 3, NPIX, NPIX)

    sim_legs = lax.map(legs_of, sims)
    data_legs = legs_of(data).astype(jnp.float32)

    def estimate(index):
        own = sim_legs[index].astype(jnp.float32)
        other = sim_legs[matching[index]].astype(jnp.float32)
        ds_x = data_legs[:, 1] * own[:, 0] + own[:, 1] * data_legs[:, 0]
        ss_x = own[:, 1] * other[:, 0] + other[:, 1] * own[:, 0]
        ds_y = data_legs[:, 2] * own[:, 0] + own[:, 2] * data_legs[:, 0]
        ss_y = own[:, 2] * other[:, 0] + other[:, 2] * own[:, 0]
        products = jnp.stack([ds_x, ss_x, ds_y, ss_y], axis=1).astype(jnp.bfloat16)
        sum_re = jnp.zeros((4, NPIX, KF), jnp.float32)
        sum_im = jnp.zeros((4, NPIX, KF), jnp.float32)
        for f in range(FIELDS):
            part_re, part_im = column_part(products[f], cos_t, sin_t)
            sum_re = sum_re + part_re.astype(jnp.float32)
            sum_im = sum_im + part_im.astype(jnp.float32)
        s_re, s_im = row_part(sum_re.astype(jnp.bfloat16), sum_im.astype(jnp.bfloat16), cos_t, sin_t)
        scale_x = ncell * lx
        scale_y = ncell * ly
        out_re = -scale_x * s_im[0:2] + -scale_y * s_im[2:4]
        out_im = scale_x * s_re[0:2] + scale_y * s_re[2:4]
        return jnp.stack([out_re, out_im], axis=1)

    return lax.map(estimate, jnp.arange(REALS, dtype=jnp.int32))
```

```python
import functools
import math

import jax
import jax.numpy as jnp
import numpy as np
from jax import lax
from jax.experimental import pallas as pl
from jax.experimental.pallas import tpu as pltpu
from jax.sharding import PartitionSpec as P

TILE = 128
LANES = 128
TAIL = 16
CHUNK = 256
BF = jnp.bfloat16
F32 = jnp.float32
VMEM_LIMIT = 60 * 1024 * 1024
MESH = pl.DeviceIdType.MESH
NT = (((1,), (1,)), ((), ()))


def round_bf(values):
    return np.asarray(values, np.float32).astype(BF)


@functools.lru_cache
def constants(npix, kf, nrows):
    top, half, h = kf // 2, npix // 2, npix // nrows
    scale, step = npix ** -0.5, 2.0 * math.pi / npix

    def cis(pixels, freqs):
        angle = np.mod(pixels[:, None] * freqs[None, :], npix) * step
        rounded = [round_bf(f(angle) * scale).astype(np.float32) for f in (np.cos, np.sin)]
        return rounded

    x, y = np.arange(half), np.arange(npix)
    fy, fx = [], []
    for kx in (np.arange(2, top + 1, 2), np.arange(1, top, 2)):
        c, s = cis(x, kx)
        lx = kx * step
        fy.append(np.concatenate([c, -s], axis=1))
        fx.append(np.concatenate([lx * s, lx * c], axis=1))
    fy, fx = np.stack(fy), np.stack(fx)
    ky = np.arange(1, top + 1)
    c, s = (v.T for v in cis(y, ky))
    ly = (ky * step)[:, None]
    zero = np.full((1, npix), round_bf(scale).astype(np.float32))
    pad = np.zeros((TAIL - 1, npix), np.float32)
    split = lambda a: a.reshape(a.shape[0], nrows, h).transpose(1, 0, 2)
    cs = split(np.concatenate([c, s, zero, pad]))
    sy = split(np.concatenate([ly * s, -ly * c, 0 * zero, pad]))
    return dict(
        fy=round_bf(fy),
        fx=round_bf(fx),
        ft=round_bf(fy.transpose(0, 2, 1)),
        cs=round_bf(cs),
        ty=round_bf(cs[:, : 2 * top].transpose(0, 2, 1)),
        ts=round_bf(np.concatenate([cs, sy], axis=2)),
        unit=float(round_bf(scale)),
        step=step,
    )


def lane_of(k, top):
    return k // 2 - 1 if k % 2 == 0 else top // 2 + (k - 1) // 2


@functools.lru_cache
def cell_tables(kf):
    top = kf // 2
    rows = np.zeros((kf + TAIL, kf), np.float32)
    cols = np.zeros((kf, kf), np.float32)
    for k in range(1, top + 1):
        if k < top:
            rows[k - 1, top + k] = 1.0
            cols[top + k, lane_of(k, top)] = 1.0
        rows[top + k - 1, top - k] = 1.0
        cols[top - k, top + lane_of(k, top)] = 1.0
    rows[kf, top] = 1.0
    return round_bf(rows), round_bf(cols)


@functools.lru_cache
def output_tables(kf, nrows):
    top, cols = kf // 2, kf // nrows
    pick = np.zeros((nrows, kf, 2 * LANES), np.float32)
    for r in range(nrows):
        for j in range(cols):
            kx = r * cols + j - top
            if kx == 0:
                continue
            lane = lane_of(abs(kx), top)
            lane = lane % (top // 2) + (lane // (top // 2)) * top
            pick[r, lane, j] = 1.0
            pick[r, lane + top // 2, LANES + j] = 1.0 if kx > 0 else -1.0
    turn = np.zeros((2, top, top), np.float32)
    for i in range(top):
        turn[0, i, top - 1 - i] = 1.0
        if i:
            turn[1, i, i - 1] = 1.0
    return round_bf(pick), round_bf(turn)


def prep_kernel(step, unit, bins_ref, own_ref, rows_ref, cols_ref, tab_ref, tabs_ref, lines_ref, ncell_ref):
    kf = cols_ref.shape[0]
    top, quarter, nbins = kf // 2, kf // 4, tab_ref.shape[1] // 2

    def take(t, idx):
        table = jnp.broadcast_to(tab_ref[t : t + 1, :], (idx.shape[0], LANES))
        parts = [
            jnp.take_along_axis(table, idx[:, i : i + LANES], axis=1, mode="promise_in_bounds")
            for i in range(0, idx.shape[1], LANES)
        ]
        return parts[0] if len(parts) == 1 else jnp.concatenate(parts, axis=1)

    by_row = jnp.dot(rows_ref[...], bins_ref[...], preferred_element_type=F32).astype(BF)
    cells = jnp.dot(by_row, cols_ref[...], preferred_element_type=F32)
    row = lax.broadcasted_iota(jnp.int32, cells.shape, 0)
    lane = lax.broadcasted_iota(jnp.int32, cells.shape, 1)
    absent = (row == top - 1) | (lane == quarter - 1)
    idx = jnp.where(absent, nbins, cells.astype(jnp.int32))
    shape = (top, top)
    ky = lax.broadcasted_iota(jnp.int32, shape, 0) + 1
    at = lax.broadcasted_iota(jnp.int32, shape, 1)
    kx = jnp.where(at < quarter, 2 * at + 2, 2 * (at - quarter) + 1)
    ly, lx = ky.astype(F32) * step, kx.astype(F32) * step
    zero_row = []
    for t in range(2):
        v = take(t, idx)
        pp, pm = v[:top, :top], v[:top, top:]
        mp, mm = v[top:kf, :top], v[top:kf, top:]
        a, b = (pp + mm) + (mp + pm), (pp + mm) - (mp + pm)
        zero_row.append(v[kf : kf + 1, :top] + v[kf : kf + 1, top:])
        if t == 0:
            tabs_ref[0] = a
            tabs_ref[1] = b
        else:
            tabs_ref[2] = lx * a
            tabs_ref[3] = lx * b
            tabs_ref[4] = ly * a
            tabs_ref[5] = ly * b
    hot = (lax.broadcasted_iota(jnp.int32, (TAIL, kf), 1) == top).astype(F32).astype(BF)
    line = lax.dot_general(hot, by_row[:kf], NT, preferred_element_type=F32)
    lane = lax.broadcasted_iota(jnp.int32, (TAIL, kf), 1)
    idx = jnp.where(lane == top - 1, nbins, line.astype(jnp.int32))
    line_w, line_g = (take(t, idx)[:1] for t in range(2))
    line_w = line_w[:, :top] + line_w[:, top:]
    line_g = line_g[:, :top] + line_g[:, top:]
    ly_row = (lax.broadcasted_iota(jnp.int32, (1, top), 1) + 1).astype(F32) * step
    dc = take(0, by_row[kf:, top : top + LANES].astype(F32).astype(jnp.int32))[:1]
    dc = jnp.where(lax.broadcasted_iota(jnp.int32, dc.shape, 1) == 0, dc * unit, 0.0)
    lines = [
        jnp.concatenate([zero_row[0] * unit, zero_row[1] * lx[:1] * unit], axis=1),
        jnp.concatenate([line_w, line_w], axis=1),
        jnp.concatenate([ly_row * line_g, -(ly_row * line_g)], axis=1),
        jnp.concatenate([dc, jnp.zeros((1, kf - LANES), F32)], axis=1),
        jnp.zeros((4, kf), F32),
    ]
    lines_ref[...] = jnp.concatenate(lines, axis=0)
    ncell_ref[...] = take(2, own_ref[...])


def prep(bins_all, own_bins, tab, kf, step, unit):
    rows, cols = cell_tables(kf)
    top = kf // 2
    vmem = pl.BlockSpec(memory_space=pltpu.VMEM)
    return pl.pallas_call(
        functools.partial(prep_kernel, step, unit),
        out_shape=[
            jax.ShapeDtypeStruct((6, top, top), F32),
            jax.ShapeDtypeStruct((8, kf), F32),
            jax.ShapeDtypeStruct(own_bins.shape, F32),
        ],
        in_specs=[vmem] * 5,
        out_specs=[vmem] * 3,
        compiler_params=pltpu.CompilerParams(vmem_limit_bytes=VMEM_LIMIT),
        cost_estimate=pl.CostEstimate(flops=4 * kf**3, bytes_accessed=16 * kf * kf, transcendentals=0),
    )(bins_all, own_bins, jnp.asarray(rows), jnp.asarray(cols), tab)


def send(src, dst, sems, at, device):
    copy = pltpu.make_async_remote_copy(
        src_ref=src,
        dst_ref=dst,
        send_sem=sems[0].at[at],
        recv_sem=sems[1].at[at],
        device_id=device,
        device_id_type=MESH,
    )
    copy.start()
    return copy


def greet(devices):
    barrier = pltpu.get_barrier_semaphore()
    for device in devices:
        pl.semaphore_signal(barrier, inc=1, device_id=device, device_id_type=MESH)
    return lambda: pl.semaphore_wait(barrier, len(devices))


def row_places(nrows):
    r = lax.axis_index("rows")
    core = lax.rem(r, 2)
    mate = {"rows": r + 1 - 2 * core}
    others = [{"rows": lax.rem(r + 2 * d, nrows)} for d in range(1, nrows // 2)]
    return r, core, mate, others


def transposed_line(columns):
    return jnp.sum(columns.T, axis=0, keepdims=True)


def as_tail(zero_row, line, corner):
    shape = (TAIL, zero_row.shape[1])
    row = lax.broadcasted_iota(jnp.int32, shape, 0)
    corner = jnp.concatenate([corner, jnp.zeros((1, shape[1] - LANES), F32)], axis=1)
    pick = lambda i, v, rest: jnp.where(row == i, jnp.broadcast_to(v, shape), rest)
    return pick(0, zero_row, pick(1, line, pick(2, corner, jnp.zeros(shape, F32))))


def store_halves(part, at, sums, tail):
    top = sums.shape[0] // 2
    for c in range(2):
        part[at, c, :top] = sums[c * top : (c + 1) * top].astype(BF)
        part[at, c, top:] = tail.astype(BF)


def lane_sums(values):
    total = values[:, :LANES]
    for i in range(LANES, values.shape[1], LANES):
        total = total + values[:, i : i + LANES]
    return total


def forward_kernel(
    nrows, unit,
    sims_ref, data_ref, mask_ref, fy_ref, cs_ref,
    out_ref,
    maps, fy, cs, even, odd, zero, cells, part, mate_in, chip, far_in,
    load_sem, s1, r1, s2, r2, s3, r3,
):
    h = maps.shape[1]
    half = even.shape[1]
    kf = cells.shape[1]
    top = kf // 2
    r, core, mate, others = row_places(nrows)
    loads = []
    for i, (src, dst) in enumerate(
        [(sims_ref, maps.at[0]), (fy_ref, fy), (cs_ref.at[r], cs), (data_ref, maps.at[1])]
    ):
        load = pltpu.make_async_copy(src, dst, load_sem.at[i])
        load.start()
        loads.append(load)
    arrived = greet([mate] + others)

    def columns(m):
        @pl.loop(0, h // TILE)
        def _(t):
            rows = pl.ds(pl.multiple_of(t * TILE, TILE), TILE)
            flags = mask_ref[t]
            lo = maps[m, rows, :half].astype(F32) * flags[:, :half]
            hi = maps[m, rows, half:].astype(F32) * flags[:, half:]
            both = lo + hi
            even[rows, :] = both.astype(BF)
            odd[rows, :] = (lo - hi).astype(BF)
            zero[rows, :] = (lane_sums(both) * unit).astype(BF)

        for q, side in enumerate((even, odd)):
            out = jnp.dot(side[...], fy[q], preferred_element_type=F32)
            cells[:, q * top : (q + 1) * top] = out.astype(BF)

    def over_rows(m):
        sums = jnp.dot(cs[...], cells[...], preferred_element_type=F32)
        line = jnp.dot(cs[...], zero[...], preferred_element_type=F32)
        tail = as_tail(sums[kf : kf + 1], transposed_line(line[:kf]), line[kf : kf + 1])
        store_halves(part, m, sums[:kf], tail)

    def to_mate(m):
        return send(part.at[m, 1 - core], mate_in.at[m], (s1, r1), m, mate)

    def to_chips(m, first):
        first.wait()
        chip[m] = (part[m, core].astype(F32) + mate_in[m].astype(F32)).astype(BF)
        return [
            send(chip.at[m], far_in.at[m, d], (s2, r2), (m, d), device)
            for d, device in enumerate(others)
        ]

    def finish(m, copies):
        total = chip[m].astype(F32)
        for d, copy in enumerate(copies):
            copy.wait()
            total = total + far_in[m, d].astype(F32)
        out_ref[m, core] = total.astype(BF)
        return send(out_ref.at[m, core], out_ref.at[m, core], (s3, r3), m, mate)

    loads[0].wait()
    loads[1].wait()
    columns(0)
    loads[2].wait()
    over_rows(0)
    arrived()
    own = to_mate(0)
    loads[3].wait()
    columns(1)
    own = to_chips(0, own)
    over_rows(1)
    data = to_mate(1)
    data = to_chips(1, data)
    own = finish(0, own)
    data = finish(1, data)
    own.wait()
    data.wait()


def forward(sims, data, mask, t, nrows, kf):
    h, npix = sims.shape
    top = kf // 2
    far = max(nrows // 2 - 1, 1)
    block = (top + TAIL, kf)
    hbm = pl.BlockSpec(memory_space=pl.ANY)
    vmem = pl.BlockSpec(memory_space=pltpu.VMEM)
    dma = pltpu.SemaphoreType.DMA
    return pl.pallas_call(
        functools.partial(forward_kernel, nrows, t["unit"]),
        out_shape=jax.ShapeDtypeStruct((2, 2) + block, BF),
        in_specs=[hbm, hbm, vmem, hbm, hbm],
        out_specs=vmem,
        scratch_shapes=[
            pltpu.VMEM((2, h, npix), BF),
            pltpu.VMEM((2, npix // 2, top), BF),
            pltpu.VMEM((kf + TAIL, h), BF),
            pltpu.VMEM((h, npix // 2), BF),
            pltpu.VMEM((h, npix // 2), BF),
            pltpu.VMEM((h, LANES), BF),
            pltpu.VMEM((h, kf), BF),
            pltpu.VMEM((2, 2) + block, BF),
            pltpu.VMEM((2,) + block, BF),
            pltpu.VMEM((2,) + block, BF),
            pltpu.VMEM((2, far) + block, BF),
            dma((4,)),
            dma((2,)), dma((2,)),
            dma((2, far)), dma((2, far)),
            dma((2,)), dma((2,)),
        ],
        compiler_params=pltpu.CompilerParams(
            collective_id=0, has_side_effects=True, vmem_limit_bytes=VMEM_LIMIT
        ),
        cost_estimate=pl.CostEstimate(
            flops=6 * h * npix * kf, bytes_accessed=6 * h * npix, transcendentals=0
        ),
    )(sims, data, mask, jnp.asarray(t["fy"]), jnp.asarray(t["cs"]))


def main_kernel(
    nrows, nreal, nfield, unit,
    pq_ref, tabs_ref, lines_ref, ncell_ref, coef_ref, ty_ref, ft_ref, fy_ref, fx_ref, ts_ref, pick_ref, turn_ref,
    out_ref,
    ty, ft, fy, fx, ts, pick, turn,
    ybuf, ycol, zbuf, own_legs, other, prods, zero, wbuf,
    zsrc, zin, psrc, pall,
    part, mate_in, chip, a_field, b_far, mid, a_far, b_field, fin,
    load_sem, sz, rz, sp, rp, s1, r1, saf, raf, sbf, rbf, say, ray, sby, rby, s3, r3,
):
    kf = wbuf.shape[1]
    top, quarter = kf // 2, kf // 4
    h = ybuf.shape[2]
    half = prods.shape[3]
    cols = out_ref.shape[3]
    r, core, mate, others = row_places(nrows)
    y = r // 2
    real = lax.axis_index("real")
    field = lax.axis_index("field")
    along_real = [{"real": lax.rem(real + d, nreal)} for d in range(1, nreal)]
    along_rows = [{"rows": lax.rem(r + d, nrows)} for d in range(1, nrows)]
    along_field = [{"field": lax.rem(field + d, nfield)} for d in range(1, nfield)]
    share = top // (nrows // 2)

    loads = []
    for i, (src, dst) in enumerate(
        [(ty_ref.at[r], ty), (ft_ref, ft), (fy_ref, fy), (fx_ref, fx), (ts_ref.at[r], ts),
         (pick_ref.at[r], pick), (turn_ref, turn)]
    ):
        load = pltpu.make_async_copy(src, dst, load_sem.at[i])
        load.start()
        loads.append(load)
    arrived = greet(along_real + along_rows + along_field)

    mine = pl.ds(pl.multiple_of(y * share, share), share)
    zsrc[:share] = pq_ref[0, core, mine, :]
    zsrc[share:] = pq_ref[0, core, top:, :]

    def make_y(pq, slot):
        tail = pq(0, top, TAIL)
        line, corner = tail[1:2], tail[2:3]
        for q in range(2):
            base = q * top
            at = slice(q * quarter, (q + 1) * quarter)
            ks = pq(0, 0, top), pq(1, 0, top)
            p_re, p_im = (ks[0][:, base + i * quarter : base + (i + 1) * quarter] for i in range(2))
            q_re, q_im = (ks[1][:, base + i * quarter : base + (i + 1) * quarter] for i in range(2))
            aw, bw, xa, xb, ya, yb = (tabs_ref[i, :, at] for i in range(6))
            sets = (
                (aw * p_re + bw * q_im, aw * p_im - bw * q_re, aw * q_re - bw * p_im, aw * q_im + bw * p_re),
                (xb * q_re - xa * p_im, xb * q_im + xa * p_re, -(xb * p_re) - xa * q_im, xa * q_re - xb * p_im),
                (ya * q_re - yb * p_im, ya * q_im + yb * p_re, -(ya * p_re) - yb * q_im, yb * q_re - ya * p_im),
            )
            for leg, values in enumerate(sets):
                for i, v in enumerate(values):
                    where = base + (i % 2) * quarter
                    zbuf[leg, (i // 2) * top : (i // 2 + 1) * top, where : where + quarter] = v.astype(BF)
        even_w, odd_w = (lines_ref[0:1, i * quarter : (i + 1) * quarter] for i in range(2))
        even_g, odd_g = (lines_ref[0:1, top + i * quarter : top + (i + 1) * quarter] for i in range(2))
        e_re, e_im, o_re, o_im = (tail[0:1, i * quarter : (i + 1) * quarter] for i in range(4))
        zero_rows = (
            jnp.concatenate([even_w * e_re, even_w * e_im, odd_w * o_re, odd_w * o_im], axis=1),
            jnp.concatenate([-(even_g * e_im), even_g * e_re, -(odd_g * o_im), odd_g * o_re], axis=1),
            None,
        )
        for leg in range(3):
            out = jnp.dot(ty[...], zbuf[leg], preferred_element_type=F32)
            if zero_rows[leg] is not None:
                out = out + zero_rows[leg]
            ybuf[slot, leg] = out.astype(BF)
        b_line = lines_ref[1:2, :] * line
        y_line = lines_ref[2:3, :] * jnp.concatenate([line[:, top:], line[:, :top]], axis=1)
        row = lax.broadcasted_iota(jnp.int32, (LANES, kf), 0)
        both = jnp.where(row == 0, b_line, jnp.where(row == 1, y_line, 0.0)).astype(BF)
        col = lax.dot_general(ty[...], both, NT, preferred_element_type=F32)
        dc = jnp.sum(corner[:, :LANES], axis=1, keepdims=True) * lines_ref[3:4, :LANES]
        ycol[slot] = (col + dc) * unit

    def make_legs(slot, dest, where, here):
        for leg in range(3):
            for q in range(2):
                out = jnp.dot(
                    ybuf[slot, leg, :, q * top : (q + 1) * top],
                    ft[q, :, here],
                    preferred_element_type=F32,
                )
                if q == 0 and leg != 1:
                    lane = 0 if leg == 0 else 1
                    out = out + ycol[slot, :, lane : lane + 1]
                dest[leg, q, :, where] = out.astype(BF)

    def make_products(here):
        rows_of = 64

        @pl.loop(0, h // rows_of)
        def _(c):
            rows = pl.ds(pl.multiple_of(c * rows_of, rows_of), rows_of)
            o = [[own_legs[leg, q, rows, here].astype(F32) for q in range(2)] for leg in range(3)]
            t = [[other[leg, q, rows, :].astype(F32) for q in range(2)] for leg in range(3)]
            for i, leg in enumerate((1, 2)):
                even = (t[leg][0] * o[0][0] + t[leg][1] * o[0][1]) + (o[leg][0] * t[0][0] + o[leg][1] * t[0][1])
                odd = (t[leg][0] * o[0][1] + t[leg][1] * o[0][0]) + (o[leg][0] * t[0][1] + o[leg][1] * t[0][0])
                prods[i, 0, rows, here] = even.astype(BF)
                prods[i, 1, rows, here] = odd.astype(BF)
                if i == 1:
                    zero[rows, :] = zero[rows, :] + lane_sums(even)

    def pair_sums(pair, slots):
        zero[...] = jnp.zeros_like(zero)

        @pl.loop(0, half // CHUNK)
        def _(c):
            here = pl.ds(pl.multiple_of(c * CHUNK, CHUNK), CHUNK)
            for slot in slots:
                if slot == 0:
                    make_legs(slot, own_legs, here, here)
                else:
                    make_legs(slot, other, slice(None), here)
            make_products(here)

        for i, table in enumerate((fx, fy)):
            for q in range(2):
                out = jnp.dot(prods[i, q], table[q], preferred_element_type=F32)
                wbuf[i * h : (i + 1) * h, q * top : (q + 1) * top] = out.astype(BF)
        sums = jnp.dot(ts[...], wbuf[...], preferred_element_type=F32)
        column = (zero[...] * unit).astype(BF)
        line = jnp.dot(ts[:, h:], column, preferred_element_type=F32)
        tail = as_tail(sums[kf : kf + 1], transposed_line(line[:kf]), jnp.zeros((1, LANES), F32))
        store_halves(part, pair, sums[:kf], tail)

    a_rows, b_rows = pl.ds(0, top // 2), pl.ds(top // 2, top // 2 + TAIL)

    def to_mate(pair):
        return send(part.at[pair, 1 - core], mate_in.at[pair], (s1, r1), pair, mate)

    def first_out(pair, copy):
        copy.wait()
        chip[pair] = (part[pair, core].astype(F32) + mate_in[pair].astype(F32)).astype(BF)
        a = [
            send(chip.at[pair, a_rows], a_field.at[pair, d], (saf, raf), (pair, d), device)
            for d, device in enumerate(along_field)
        ]
        b = [
            send(chip.at[pair, b_rows], b_far.at[pair, d], (sby, rby), (pair, d), device)
            for d, device in enumerate(others)
        ]
        return a, b

    def gathered(total, copies, slots):
        total = total.astype(F32)
        for d, copy in enumerate(copies):
            copy.wait()
            total = total + slots(d).astype(F32)
        return total.astype(BF)

    def second_out(pair, copies):
        a, b = copies
        mid[pair, a_rows] = gathered(chip[pair, a_rows], a, lambda d: a_field[pair, d])
        a = [
            send(mid.at[pair, a_rows], a_far.at[pair, d], (say, ray), (pair, d), device)
            for d, device in enumerate(others)
        ]
        mid[pair, b_rows] = gathered(chip[pair, b_rows], b, lambda d: b_far[pair, d])
        b = [
            send(mid.at[pair, b_rows], b_field.at[pair, d], (sbf, rbf), (pair, d), device)
            for d, device in enumerate(along_field)
        ]
        return a, b

    def last_out(pair, copies):
        a, b = copies
        fin[pair, core, a_rows] = gathered(mid[pair, a_rows], a, lambda d: a_far[pair, d])
        fin[pair, core, b_rows] = gathered(mid[pair, b_rows], b, lambda d: b_field[pair, d])
        return send(fin.at[pair, core], fin.at[pair, core], (s3, r3), pair, mate)

    def assemble(pair, copy):
        copy.wait()
        picked = [
            jnp.dot(fin[pair, c, :top], pick[...], preferred_element_type=F32) for c in range(2)
        ]
        tail = fin[pair, 0, top:]
        zero_line = jnp.dot(tail, pick[...], preferred_element_type=F32)[:1]
        column = jnp.broadcast_to(tail.astype(F32)[1:2], (LANES, kf)).T
        lane = lax.broadcasted_iota(jnp.int32, (kf, LANES), 1)
        column = jnp.where(lane + r * cols == top, column, 0.0)
        p_re, p_im = picked[0][:, :LANES] + column[:top], picked[0][:, LANES:]
        q_re, q_im = picked[1][:, :LANES] + column[top:], picked[1][:, LANES:]
        plus = jnp.concatenate([p_re + q_im, p_im - q_re], axis=1).astype(BF)
        minus = jnp.concatenate([p_re - q_im, p_im + q_re], axis=1).astype(BF)
        lower = jnp.dot(turn[0], minus, preferred_element_type=F32)
        upper = jnp.dot(turn[1], plus, preferred_element_type=F32)
        row = lax.broadcasted_iota(jnp.int32, upper.shape, 0)
        upper = jnp.where(row == 0, zero_line, upper)
        for i in range(2):
            at = slice(i * LANES, i * LANES + cols)
            out_ref[pair, i, :top] = lower[:, at] * ncell_ref[:top]
            out_ref[pair, i, top:] = upper[:, at] * ncell_ref[top:]

    arrived()
    z_copies = [
        send(zsrc, zin.at[d], (sz, rz), d, device) for d, device in enumerate(along_real)
    ]
    loads[0].wait()
    make_y(lambda c, at, n: pq_ref[0, c, at : at + n].astype(F32), 0)
    make_y(lambda c, at, n: pq_ref[1, c, at : at + n].astype(F32), 1)
    for load in loads[1:]:
        load.wait()
    pair_sums(0, (0, 1))
    ds = to_mate(0)
    partner = coef_ref[0:1, 0:1] * zsrc[...].astype(F32)
    for d, copy in enumerate(z_copies):
        copy.wait()
        partner = partner + coef_ref[d + 1 : d + 2, 0:1] * zin[d].astype(F32)
    partner = partner.astype(BF)
    psrc[...] = partner[:share]
    pall[core, mine, :] = partner[:share]
    for c in range(2):
        pall[c, top:, :] = partner[share:]
    p_copies = [
        send(psrc, pall.at[core, mine], (sp, rp), d, device) for d, device in enumerate(along_rows)
    ]
    ds = first_out(0, ds)
    for copy in p_copies:
        copy.wait()
    make_y(lambda c, at, n: pall[c, at : at + n].astype(F32), 1)
    ds = second_out(0, ds)
    pair_sums(1, (1,))
    ss = to_mate(1)
    ds = last_out(0, ds)
    ss = first_out(1, ss)
    assemble(0, ds)
    ss = second_out(1, ss)
    ss = last_out(1, ss)
    assemble(1, ss)


def estimate(pq, tabs, lines, ncell, coef, t, nrows, nreal, nfield):
    kf, cols = ncell.shape
    top = kf // 2
    npix = t["cs"].shape[2] * nrows
    h, half = npix // nrows, npix // 2
    far, fields = max(nrows // 2 - 1, 1), max(nfield - 1, 1)
    share = top // (nrows // 2)
    pick, turn = output_tables(kf, nrows)
    hbm = pl.BlockSpec(memory_space=pl.ANY)
    vmem = pl.BlockSpec(memory_space=pltpu.VMEM)
    dma = pltpu.SemaphoreType.DMA
    block = (top + TAIL, kf)
    a_block, b_block = (top // 2, kf), (top // 2 + TAIL, kf)
    buf = lambda *shape: pltpu.VMEM(shape, BF)
    return pl.pallas_call(
        functools.partial(main_kernel, nrows, nreal, nfield, t["unit"]),
        out_shape=jax.ShapeDtypeStruct((2, 2, kf, cols), F32),
        in_specs=[vmem] * 5 + [hbm] * 7,
        out_specs=vmem,
        scratch_shapes=[
            buf(h, kf), buf(2, top, half), buf(2, half, top), buf(2, half, top), buf(kf + TAIL, 2 * h),
            buf(kf, 2 * LANES), buf(2, top, top),
            buf(2, 3, h, kf), pltpu.VMEM((2, h, LANES), F32), buf(3, kf, kf),
            buf(3, 2, h, half), buf(3, 2, h, CHUNK), buf(2, 2, h, half),
            pltpu.VMEM((h, LANES), F32), buf(2 * h, kf),
            buf(share + TAIL, kf), buf(nreal - 1, share + TAIL, kf), buf(share, kf), buf(2, *block),
            buf(2, 2, *block), buf(2, *block), buf(2, *block),
            buf(2, fields, *a_block), buf(2, far, *b_block), buf(2, *block),
            buf(2, far, *a_block), buf(2, fields, *b_block), buf(2, 2, *block),
            dma((7,)),
            dma((nreal - 1,)), dma((nreal - 1,)),
            dma((nrows - 1,)), dma((nrows - 1,)),
            dma((2,)), dma((2,)),
            dma((2, fields)), dma((2, fields)),
            dma((2, fields)), dma((2, fields)),
            dma((2, far)), dma((2, far)),
            dma((2, far)), dma((2, far)),
            dma((2,)), dma((2,)),
        ],
        compiler_params=pltpu.CompilerParams(
            collective_id=1, has_side_effects=True, vmem_limit_bytes=VMEM_LIMIT
        ),
        cost_estimate=pl.CostEstimate(
            flops=26 * h * npix * kf, bytes_accessed=16 * 2**20, transcendentals=0
        ),
    )(
        pq, tabs, lines, ncell, coef,
        *(jnp.asarray(t[name]) for name in ("ty", "ft", "fy", "fx", "ts")),
        jnp.asarray(pick), jnp.asarray(turn),
    )


def body(nrows, nreal, nfield, sims, data, mask_flags, bins, cl_signal, cl_noise, norm, matching):
    npix = sims.shape[3]
    kf, cols = bins.shape
    t = constants(npix, kf, nrows)
    mask = jnp.repeat(mask_flags.astype(F32), TILE, axis=1)[:, None, :]
    bins_all = lax.all_gather(bins.astype(BF), "rows", axis=1, tiled=True)
    weight = 1.0 / (cl_signal[0] + cl_noise[0])
    nbins = norm.shape[0]
    tab = jnp.stack([4.0 * weight, 4.0 * (cl_signal[0] * weight), 2.0 * norm])
    tab = jnp.pad(tab, ((0, 5), (0, LANES - nbins)))
    real = lax.axis_index("real")
    partner = jnp.sum(jnp.where(jnp.arange(nreal) == real, matching, 0))
    coef = (lax.rem(real - jnp.arange(nreal) + nreal, nreal) == partner).astype(F32)
    coef = jnp.broadcast_to(coef[:, None], (nreal, LANES))
    pq = forward(sims[0, 0], data[0], mask, t, nrows, kf)
    tabs, lines, ncell = prep(bins_all, bins, tab, kf, t["step"], t["unit"])
    return estimate(pq, tabs, lines, ncell, coef, t, nrows, nreal, nfield)[None]


def solution(mesh):
    in_specs = (
        P("real", "field", "rows", None),
        P("field", "rows", None),
        P("rows", None),
        P(None, "rows"),
        P("field", None),
        P("field", None),
        P(),
        P(),
    )
    out_specs = P("real", None, None, None, "rows")
    f = functools.partial(body, mesh.shape["rows"], mesh.shape["real"], mesh.shape["field"])
    return jax.shard_map(f, mesh=mesh, in_specs=in_specs, out_specs=out_specs, check_vma=False)
```

```python
import functools
import math
import types

import jax
import jax.numpy as jnp
import numpy as np
from jax import lax
from jax.experimental import pallas as pl
from jax.experimental.pallas import tpu as pltpu
from jax.sharding import PartitionSpec as P

TILE = 128
LANES = 128
TAIL = 16
CHUNK = 256
BF = jnp.bfloat16
F32 = jnp.float32
VMEM_LIMIT = 60 * 1024 * 1024
MESH = pl.DeviceIdType.MESH
NT = (((1,), (1,)), ((), ()))


def round_bf(values):
    return np.asarray(values, np.float32).astype(BF)


@functools.lru_cache
def constants(npix, kf, nrows):
    top, half, h = kf // 2, npix // 2, npix // nrows
    scale, step = npix ** -0.5, 2.0 * math.pi / npix

    def cis(pixels, freqs):
        angle = np.mod(pixels[:, None] * freqs[None, :], npix) * step
        rounded = [round_bf(f(angle) * scale).astype(np.float32) for f in (np.cos, np.sin)]
        return rounded

    x, y = np.arange(half), np.arange(npix)
    fy, fx = [], []
    for kx in (np.arange(2, top + 1, 2), np.arange(1, top, 2)):
        c, s = cis(x, kx)
        lx = kx * step
        fy.append(np.concatenate([c, -s], axis=1))
        fx.append(np.concatenate([lx * s, lx * c], axis=1))
    fy, fx = np.stack(fy), np.stack(fx)
    ky = np.arange(1, top + 1)
    c, s = (v.T for v in cis(y, ky))
    ly = (ky * step)[:, None]
    zero = np.full((1, npix), round_bf(scale).astype(np.float32))
    pad = np.zeros((TAIL - 1, npix), np.float32)
    split = lambda a: a.reshape(a.shape[0], nrows, h).transpose(1, 0, 2)
    cs = split(np.concatenate([c, s, zero, pad]))
    sy = split(np.concatenate([ly * s, -ly * c, 0 * zero, pad]))
    return dict(
        fy=round_bf(fy),
        fx=round_bf(fx),
        ft=round_bf(fy.transpose(0, 2, 1)),
        cs=round_bf(cs),
        ty=round_bf(cs[:, : 2 * top].transpose(0, 2, 1)),
        ts=round_bf(np.concatenate([cs, sy], axis=2)),
        unit=float(round_bf(scale)),
        step=step,
    )


def lane_of(k, top):
    return k // 2 - 1 if k % 2 == 0 else top // 2 + (k - 1) // 2


@functools.lru_cache
def cell_tables(kf):
    top = kf // 2
    rows = np.zeros((kf + TAIL, kf), np.float32)
    cols = np.zeros((kf, kf), np.float32)
    for k in range(1, top + 1):
        if k < top:
            rows[k - 1, top + k] = 1.0
            cols[top + k, lane_of(k, top)] = 1.0
        rows[top + k - 1, top - k] = 1.0
        cols[top - k, top + lane_of(k, top)] = 1.0
    rows[kf, top] = 1.0
    return round_bf(rows), round_bf(cols)


@functools.lru_cache
def output_tables(kf, nrows):
    top, cols = kf // 2, kf // nrows
    pick = np.zeros((nrows, kf, 2 * LANES), np.float32)
    for r in range(nrows):
        for j in range(cols):
            kx = r * cols + j - top
            if kx == 0:
                continue
            lane = lane_of(abs(kx), top)
            lane = lane % (top // 2) + (lane // (top // 2)) * top
            pick[r, lane, j] = 1.0
            pick[r, lane + top // 2, LANES + j] = 1.0 if kx > 0 else -1.0
    turn = np.zeros((2, top, top), np.float32)
    for i in range(top):
        turn[0, i, top - 1 - i] = 1.0
        if i:
            turn[1, i, i - 1] = 1.0
    return round_bf(pick), round_bf(turn)


def send(src, dst, sems, at, device):
    copy = pltpu.make_async_remote_copy(
        src_ref=src,
        dst_ref=dst,
        send_sem=sems[0].at[at],
        recv_sem=sems[1].at[at],
        device_id=device,
        device_id_type=MESH,
    )
    copy.start()
    return copy


def greet(devices):
    barrier = pltpu.get_barrier_semaphore()
    for device in devices:
        pl.semaphore_signal(barrier, inc=1, device_id=device, device_id_type=MESH)
    return lambda: pl.semaphore_wait(barrier, len(devices))


def row_places(nrows):
    r = lax.axis_index("rows")
    core = lax.rem(r, 2)
    mate = {"rows": r + 1 - 2 * core}
    others = [{"rows": lax.rem(r + 2 * d, nrows)} for d in range(1, nrows // 2)]
    return r, core, mate, others


def expanded(flags):
    rows, tiles = flags.shape
    return jnp.concatenate(
        [jnp.broadcast_to(flags[:, j : j + 1], (rows, TILE)) for j in range(tiles)], axis=1
    )


def transposed_line(columns):
    return jnp.sum(columns.T, axis=0, keepdims=True)


def as_tail(zero_row, line, corner):
    shape = (TAIL, zero_row.shape[1])
    row = lax.broadcasted_iota(jnp.int32, shape, 0)
    corner = jnp.concatenate([corner, jnp.zeros((1, shape[1] - LANES), F32)], axis=1)
    pick = lambda i, v, rest: jnp.where(row == i, jnp.broadcast_to(v, shape), rest)
    return pick(0, zero_row, pick(1, line, pick(2, corner, jnp.zeros(shape, F32))))


def store_halves(part, at, sums, tail):
    top = sums.shape[0] // 2
    for c in range(2):
        part[at, c, :top] = sums[c * top : (c + 1) * top].astype(BF)
        part[at, c, top:] = tail.astype(BF)


def lane_sums(values):
    total = values[:, :LANES]
    for i in range(LANES, values.shape[1], LANES):
        total = total + values[:, i : i + LANES]
    return total


def kernel(
    sizes, names,
    sims_ref, data_ref, mask_ref, bins_ref, signal_ref, noise_ref, norm_ref, matching_ref,
    fy_ref, cs_ref, rows_ref, cols_ref, ty_ref, ft_ref, fx_ref, ts_ref, pick_ref, turn_ref,
    out_ref, ncell_ref,
    *scratch,
):
    nrows, nreal, nfield, unit, step = sizes
    s = types.SimpleNamespace(**dict(zip(names, scratch)))
    h, kf = s.cells.shape
    top, quarter, half = kf // 2, kf // 4, s.even.shape[1]
    cols = ncell_ref.shape[1]
    nbins = norm_ref.shape[1]
    r, core, mate, others = row_places(nrows)
    y, chips = r // 2, nrows // 2
    real = lax.axis_index("real")
    field = lax.axis_index("field")
    along_real = [{"real": lax.rem(real + d, nreal)} for d in range(1, nreal)]
    along_rows = [{"rows": lax.rem(r + d, nrows)} for d in range(1, nrows)]
    along_field = [{"field": lax.rem(field + d, nfield)} for d in range(1, nfield)]
    share = top // chips
    mine = pl.ds(pl.multiple_of(y * share, share), share)

    loads = {}
    for i, (name, src, dst) in enumerate(
        [("own", sims_ref, s.maps.at[0]), ("fy", fy_ref, s.fy), ("cs", cs_ref.at[r], s.cs),
         ("data", data_ref, s.maps.at[1]), ("rows", rows_ref, s.rows), ("cols", cols_ref, s.cols),
         ("ty", ty_ref.at[r], s.ty), ("ft", ft_ref, s.ft), ("fx", fx_ref, s.fx),
         ("ts", ts_ref.at[r], s.ts), ("pick", pick_ref.at[r], s.pick), ("turn", turn_ref, s.turn)]
    ):
        loads[name] = pltpu.make_async_copy(src, dst, s.load_sem.at[i])
        loads[name].start()
    arrived = greet(along_real + along_rows + along_field)


    def bins_out():
        s.bins[r] = bins_ref[...].astype(F32).astype(BF)
        return [
            send(s.bins.at[r], s.bins.at[r], (s.sbf, s.rbf), d, device)
            for d, device in enumerate(others)
        ]

    def bins_on(copies):
        for copy in copies:
            copy.wait()
        blocks = [lax.rem(r + 2 * d, nrows) for d in range(chips)]
        return [
            send(s.bins.at[block], s.bins.at[block], (s.sbm, s.rbm), d, mate)
            for d, block in enumerate(blocks)
        ]

    def take(t, idx):
        table = jnp.broadcast_to(s.tab[t : t + 1, :], (idx.shape[0], LANES))
        parts = [
            jnp.take_along_axis(table[:, : idx.shape[1]] if idx.shape[1] < LANES else table,
                                idx[:, i : i + LANES], axis=1, mode="promise_in_bounds")
            for i in range(0, idx.shape[1], LANES)
        ]
        return parts[0] if len(parts) == 1 else jnp.concatenate(parts, axis=1)

    def filters():
        weight = 1.0 / (signal_ref[...] + noise_ref[...])
        s.tab[...] = jnp.zeros_like(s.tab)
        s.tab[0:1, :nbins] = 4.0 * weight
        s.tab[1:2, :nbins] = 4.0 * (signal_ref[...] * weight)
        s.tab[2:3, :nbins] = 2.0 * norm_ref[...]
        ncell_ref[...] = take(2, bins_ref[...])
        by_row = [
            jnp.dot(s.rows[...], s.bins[i], preferred_element_type=F32).astype(BF) for i in range(nrows)
        ]
        by_row = jnp.concatenate(by_row, axis=1)
        cells = jnp.dot(by_row, s.cols[...], preferred_element_type=F32)
        row = lax.broadcasted_iota(jnp.int32, cells.shape, 0)
        lane = lax.broadcasted_iota(jnp.int32, cells.shape, 1)
        absent = (row == top - 1) | (lane == quarter - 1)
        idx = jnp.where(absent, nbins, cells.astype(jnp.int32))
        shape = (top, top)
        ky = lax.broadcasted_iota(jnp.int32, shape, 0) + 1
        at = lax.broadcasted_iota(jnp.int32, shape, 1)
        kx = jnp.where(at < quarter, 2 * at + 2, 2 * (at - quarter) + 1)
        ly, lx = ky.astype(F32) * step, kx.astype(F32) * step
        zero_row = []
        for t in range(2):
            v = take(t, idx)
            pp, pm = v[:top, :top], v[:top, top:]
            mp, mm = v[top:kf, :top], v[top:kf, top:]
            a, b = (pp + mm) + (mp + pm), (pp + mm) - (mp + pm)
            zero_row.append(v[kf : kf + 1, :top] + v[kf : kf + 1, top:])
            if t == 0:
                s.tabs[0] = a
                s.tabs[1] = b
            else:
                s.tabs[2] = lx * a
                s.tabs[3] = lx * b
                s.tabs[4] = ly * a
                s.tabs[5] = ly * b
        hot = (lax.broadcasted_iota(jnp.int32, (TAIL, kf), 1) == top).astype(F32).astype(BF)
        line = lax.dot_general(hot, by_row[:kf], NT, preferred_element_type=F32)
        lane = lax.broadcasted_iota(jnp.int32, (TAIL, kf), 1)
        idx = jnp.where(lane == top - 1, nbins, line.astype(jnp.int32))
        line_w, line_g = (take(t, idx)[:1] for t in range(2))
        line_w = line_w[:, :top] + line_w[:, top:]
        line_g = line_g[:, :top] + line_g[:, top:]
        ly_row = (lax.broadcasted_iota(jnp.int32, (1, top), 1) + 1).astype(F32) * step
        dc = take(0, by_row[kf:, top : top + LANES].astype(F32).astype(jnp.int32))[:1]
        dc = jnp.where(lax.broadcasted_iota(jnp.int32, dc.shape, 1) == 0, dc * unit, 0.0)
        lines = [
            jnp.concatenate([zero_row[0] * unit, zero_row[1] * lx[:1] * unit], axis=1),
            jnp.concatenate([line_w, line_w], axis=1),
            jnp.concatenate([ly_row * line_g, -(ly_row * line_g)], axis=1),
            jnp.concatenate([dc, jnp.zeros((1, kf - LANES), F32)], axis=1),
            jnp.zeros((4, kf), F32),
        ]
        s.lines[...] = jnp.concatenate(lines, axis=0)


    def columns(m):
        @pl.loop(0, h // TILE)
        def _(t):
            rows = pl.ds(pl.multiple_of(t * TILE, TILE), TILE)
            flags = s.mask[t]
            lo = s.maps[m, rows, :half].astype(F32) * flags[:, :half]
            hi = s.maps[m, rows, half:].astype(F32) * flags[:, half:]
            both = lo + hi
            s.even[rows, :] = both.astype(BF)
            s.odd[rows, :] = (lo - hi).astype(BF)
            s.zero_b[rows, :] = (lane_sums(both) * unit).astype(BF)

        for q, side in enumerate((s.even, s.odd)):
            out = jnp.dot(side[...], s.fy[q], preferred_element_type=F32)
            s.cells[:, q * top : (q + 1) * top] = out.astype(BF)

    def over_rows(m):
        sums = jnp.dot(s.cs[...], s.cells[...], preferred_element_type=F32)
        line = jnp.dot(s.cs[...], s.zero_b[...], preferred_element_type=F32)
        tail = as_tail(sums[kf : kf + 1], transposed_line(line[:kf]), line[kf : kf + 1])
        store_halves(s.fpart, m, sums[:kf], tail)

    def cells_to_mate(m):
        return send(s.fpart.at[m, 1 - core], s.fmate.at[m], (s.sf1, s.rf1), m, mate)

    def cells_to_chips(m, first):
        first.wait()
        s.fchip[m] = (s.fpart[m, core].astype(F32) + s.fmate[m].astype(F32)).astype(BF)
        return [
            send(s.fchip.at[m], s.ffar.at[m, d], (s.sf2, s.rf2), (m, d), device)
            for d, device in enumerate(others)
        ]

    def cells_done(m, copies):
        total = s.fchip[m].astype(F32)
        for d, copy in enumerate(copies):
            copy.wait()
            total = total + s.ffar[m, d].astype(F32)
        s.pq[m, core] = total.astype(BF)
        return send(s.pq.at[m, core], s.pq.at[m, core], (s.sf3, s.rf3), m, mate)


    def partner_out():
        s.zsrc[:share] = s.pq[0, core, mine, :]
        s.zsrc[share:] = s.pq[0, core, top:, :]
        return [
            send(s.zsrc, s.zin.at[d], (s.sz, s.rz), d, device) for d, device in enumerate(along_real)
        ]

    def partner_on(copies):
        partner = matching_ref[real]
        named = lambda d: jnp.where(lax.rem(real - d + nreal, nreal) == partner, 1.0, 0.0)
        total = named(0) * s.zsrc[...].astype(F32)
        for d, copy in enumerate(copies):
            copy.wait()
            total = total + named(d + 1) * s.zin[d].astype(F32)
        total = total.astype(BF)
        s.psrc[...] = total[:share]
        s.pall[core, mine, :] = total[:share]
        for c in range(2):
            s.pall[c, top:, :] = total[share:]
        return [
            send(s.psrc, s.pall.at[core, mine], (s.sp, s.rp), d, device)
            for d, device in enumerate(along_rows)
        ]

    def make_y(pq, slot):
        tail = pq(0, top, TAIL)
        line, corner = tail[1:2], tail[2:3]
        for q in range(2):
            base = q * top
            at = slice(q * quarter, (q + 1) * quarter)
            ks = pq(0, 0, top), pq(1, 0, top)
            p_re, p_im = (ks[0][:, base + i * quarter : base + (i + 1) * quarter] for i in range(2))
            q_re, q_im = (ks[1][:, base + i * quarter : base + (i + 1) * quarter] for i in range(2))
            aw, bw, xa, xb, ya, yb = (s.tabs[i, :, at] for i in range(6))
            sets = (
                (aw * p_re + bw * q_im, aw * p_im - bw * q_re, aw * q_re - bw * p_im, aw * q_im + bw * p_re),
                (xb * q_re - xa * p_im, xb * q_im + xa * p_re, -(xb * p_re) - xa * q_im, xa * q_re - xb * p_im),
                (ya * q_re - yb * p_im, ya * q_im + yb * p_re, -(ya * p_re) - yb * q_im, yb * q_re - ya * p_im),
            )
            for leg, values in enumerate(sets):
                for i, v in enumerate(values):
                    where = base + (i % 2) * quarter
                    s.zbuf[leg, (i // 2) * top : (i // 2 + 1) * top, where : where + quarter] = v.astype(BF)
        even_w, odd_w = (s.lines[0:1, i * quarter : (i + 1) * quarter] for i in range(2))
        even_g, odd_g = (s.lines[0:1, top + i * quarter : top + (i + 1) * quarter] for i in range(2))
        e_re, e_im, o_re, o_im = (tail[0:1, i * quarter : (i + 1) * quarter] for i in range(4))
        zero_rows = (
            jnp.concatenate([even_w * e_re, even_w * e_im, odd_w * o_re, odd_w * o_im], axis=1),
            jnp.concatenate([-(even_g * e_im), even_g * e_re, -(odd_g * o_im), odd_g * o_re], axis=1),
            None,
        )
        for leg in range(3):
            out = jnp.dot(s.ty[...], s.zbuf[leg], preferred_element_type=F32)
            if zero_rows[leg] is not None:
                out = out + zero_rows[leg]
            s.ybuf[slot, leg] = out.astype(BF)
        b_line = s.lines[1:2, :] * line
        y_line = s.lines[2:3, :] * jnp.concatenate([line[:, top:], line[:, :top]], axis=1)
        row = lax.broadcasted_iota(jnp.int32, (LANES, kf), 0)
        both = jnp.where(row == 0, b_line, jnp.where(row == 1, y_line, 0.0)).astype(BF)
        col = lax.dot_general(s.ty[...], both, NT, preferred_element_type=F32)
        dc = jnp.sum(corner[:, :LANES], axis=1, keepdims=True) * s.lines[3:4, :LANES]
        s.ycol[slot] = (col + dc) * unit

    def make_legs(slot, dest, where, here):
        for leg in range(3):
            for q in range(2):
                out = jnp.dot(
                    s.ybuf[slot, leg, :, q * top : (q + 1) * top],
                    s.ft[q, :, here],
                    preferred_element_type=F32,
                )
                if q == 0 and leg != 1:
                    lane = 0 if leg == 0 else 1
                    out = out + s.ycol[slot, :, lane : lane + 1]
                dest[leg, q, :, where] = out.astype(BF)

    def make_products(here):
        rows_of = 64

        @pl.loop(0, h // rows_of)
        def _(c):
            rows = pl.ds(pl.multiple_of(c * rows_of, rows_of), rows_of)
            o = [[s.own_legs[leg, q, rows, here].astype(F32) for q in range(2)] for leg in range(3)]
            t = [[s.other[leg, q, rows, :].astype(F32) for q in range(2)] for leg in range(3)]
            for i, leg in enumerate((1, 2)):
                even = (t[leg][0] * o[0][0] + t[leg][1] * o[0][1]) + (o[leg][0] * t[0][0] + o[leg][1] * t[0][1])
                odd = (t[leg][0] * o[0][1] + t[leg][1] * o[0][0]) + (o[leg][0] * t[0][1] + o[leg][1] * t[0][0])
                s.prods[i, 0, rows, here] = even.astype(BF)
                s.prods[i, 1, rows, here] = odd.astype(BF)
                if i == 1:
                    s.zero[rows, :] = s.zero[rows, :] + lane_sums(even)

    def own_done():
        @pl.loop(0, half // CHUNK)
        def _(c):
            here = pl.ds(pl.multiple_of(c * CHUNK, CHUNK), CHUNK)
            make_legs(0, s.own_legs, here, here)

    def pair_products():
        s.zero[...] = jnp.zeros_like(s.zero)

        @pl.loop(0, half // CHUNK)
        def _(c):
            here = pl.ds(pl.multiple_of(c * CHUNK, CHUNK), CHUNK)
            make_legs(1, s.other, slice(None), here)
            make_products(here)

    def pair_sums(pair):
        for i, table in enumerate((s.fx, s.fy)):
            for q in range(2):
                out = jnp.dot(s.prods[i, q], table[q], preferred_element_type=F32)
                s.wbuf[i * h : (i + 1) * h, q * top : (q + 1) * top] = out.astype(BF)
        sums = jnp.dot(s.ts[...], s.wbuf[...], preferred_element_type=F32)
        column = (s.zero[...] * unit).astype(BF)
        line = jnp.dot(s.ts[:, h:], column, preferred_element_type=F32)
        tail = as_tail(sums[kf : kf + 1], transposed_line(line[:kf]), jnp.zeros((1, LANES), F32))
        store_halves(s.part, pair, sums[:kf], tail)

    a_rows, b_rows = pl.ds(0, top // 2), pl.ds(top // 2, top // 2 + TAIL)

    def to_mate(pair):
        return send(s.part.at[pair, 1 - core], s.mate_in.at[pair], (s.s1, s.r1), pair, mate)

    def first_out(pair, copy):
        copy.wait()
        s.chip[pair] = (s.part[pair, core].astype(F32) + s.mate_in[pair].astype(F32)).astype(BF)
        a = [
            send(s.chip.at[pair, a_rows], s.a_field.at[pair, d], (s.saf, s.raf), (pair, d), device)
            for d, device in enumerate(along_field)
        ]
        b = [
            send(s.chip.at[pair, b_rows], s.b_far.at[pair, d], (s.sby, s.rby), (pair, d), device)
            for d, device in enumerate(others)
        ]
        return a, b

    def gathered(total, copies, slots):
        total = total.astype(F32)
        for d, copy in enumerate(copies):
            copy.wait()
            total = total + slots(d).astype(F32)
        return total.astype(BF)

    def second_out(pair, copies):
        a, b = copies
        s.mid[pair, a_rows] = gathered(s.chip[pair, a_rows], a, lambda d: s.a_field[pair, d])
        a = [
            send(s.mid.at[pair, a_rows], s.a_far.at[pair, d], (s.say, s.ray), (pair, d), device)
            for d, device in enumerate(others)
        ]
        s.mid[pair, b_rows] = gathered(s.chip[pair, b_rows], b, lambda d: s.b_far[pair, d])
        b = [
            send(s.mid.at[pair, b_rows], s.b_field.at[pair, d], (s.sbfield, s.rbfield), (pair, d), device)
            for d, device in enumerate(along_field)
        ]
        return a, b

    def last_out(pair, copies):
        a, b = copies
        s.fin[pair, core, a_rows] = gathered(s.mid[pair, a_rows], a, lambda d: s.a_far[pair, d])
        s.fin[pair, core, b_rows] = gathered(s.mid[pair, b_rows], b, lambda d: s.b_field[pair, d])
        return send(s.fin.at[pair, core], s.fin.at[pair, core], (s.s3, s.r3), pair, mate)

    def assemble(pair, copy):
        copy.wait()
        picked = [
            jnp.dot(s.fin[pair, c, :top], s.pick[...], preferred_element_type=F32) for c in range(2)
        ]
        tail = s.fin[pair, 0, top:]
        zero_line = jnp.dot(tail, s.pick[...], preferred_element_type=F32)[:1]
        column = jnp.broadcast_to(tail.astype(F32)[1:2], (LANES, kf)).T
        lane = lax.broadcasted_iota(jnp.int32, (kf, LANES), 1)
        column = jnp.where(lane + r * cols == top, column, 0.0)
        p_re, p_im = picked[0][:, :LANES] + column[:top], picked[0][:, LANES:]
        q_re, q_im = picked[1][:, :LANES] + column[top:], picked[1][:, LANES:]
        plus = jnp.concatenate([p_re + q_im, p_im - q_re], axis=1).astype(BF)
        minus = jnp.concatenate([p_re - q_im, p_im + q_re], axis=1).astype(BF)
        lower = jnp.dot(s.turn[0], minus, preferred_element_type=F32)
        upper = jnp.dot(s.turn[1], plus, preferred_element_type=F32)
        row = lax.broadcasted_iota(jnp.int32, upper.shape, 0)
        upper = jnp.where(row == 0, zero_line, upper)
        for i in range(2):
            at = slice(i * LANES, i * LANES + cols)
            out_ref[pair, i, :top] = lower[:, at]
            out_ref[pair, i, top:] = upper[:, at]

    full = expanded(mask_ref[...].astype(F32))
    for t in range(full.shape[0]):
        s.mask[t] = full[t : t + 1]
    loads["own"].wait()
    loads["fy"].wait()
    columns(0)
    arrived()
    bins = bins_out()
    loads["cs"].wait()
    over_rows(0)
    own = cells_to_mate(0)
    loads["data"].wait()
    columns(1)
    own = cells_to_chips(0, own)
    bins = bins_on(bins)
    over_rows(1)
    data = cells_to_mate(1)
    for name in ("rows", "cols", "ty", "ft", "fx", "ts", "pick", "turn"):
        loads[name].wait()
    data = cells_to_chips(1, data)
    for copy in bins:
        copy.wait()
    filters()
    own = cells_done(0, own)
    partner = partner_out()
    own.wait()
    make_y(lambda c, at, n: s.pq[0, c, at : at + n].astype(F32), 0)
    own_done()
    data = cells_done(1, data)
    data.wait()
    make_y(lambda c, at, n: s.pq[1, c, at : at + n].astype(F32), 1)
    pair_products()
    partner = partner_on(partner)
    pair_sums(0)
    ds = to_mate(0)
    for copy in partner:
        copy.wait()
    make_y(lambda c, at, n: s.pall[c, at : at + n].astype(F32), 1)
    ds = first_out(0, ds)
    pair_products()
    ds = second_out(0, ds)
    pair_sums(1)
    ss = to_mate(1)
    ds = last_out(0, ds)
    ss = first_out(1, ss)
    assemble(0, ds)
    ss = second_out(1, ss)
    ss = last_out(1, ss)
    assemble(1, ss)


def estimates(sims, data, mask_flags, bins, signal, noise, norm, matching, nrows, nreal, nfield):
    h, npix = sims.shape
    kf, cols = bins.shape
    top, half = kf // 2, npix // 2
    t = constants(npix, kf, nrows)
    rows, pick_cols = cell_tables(kf)
    pick, turn = output_tables(kf, nrows)
    far, fields = max(nrows // 2 - 1, 1), max(nfield - 1, 1)
    share = top // (nrows // 2)
    block = (top + TAIL, kf)
    a_block, b_block = (top // 2, kf), (top // 2 + TAIL, kf)
    buf = lambda *shape: pltpu.VMEM(shape, BF)
    wide = lambda *shape: pltpu.VMEM(shape, F32)
    dma = lambda *shape: pltpu.SemaphoreType.DMA(shape)
    scratch = dict(
        maps=buf(2, h, npix), fy=buf(2, half, top), cs=buf(kf + TAIL, h), rows=buf(kf + TAIL, kf),
        cols=buf(kf, kf), ty=buf(h, kf), ft=buf(2, top, half), fx=buf(2, half, top),
        ts=buf(kf + TAIL, 2 * h), pick=buf(kf, 2 * LANES), turn=buf(2, top, top),
        mask=wide(h // TILE, 1, npix), bins=buf(nrows, kf, cols), tab=wide(8, LANES),
        tabs=wide(6, top, top), lines=wide(8, kf),
        even=buf(h, half), odd=buf(h, half), zero_b=buf(h, LANES), cells=buf(h, kf),
        fpart=buf(2, 2, *block), fmate=buf(2, *block), fchip=buf(2, *block), ffar=buf(2, far, *block),
        pq=buf(2, 2, *block),
        zsrc=buf(share + TAIL, kf), zin=buf(nreal - 1, share + TAIL, kf), psrc=buf(share, kf),
        pall=buf(2, *block),
        ybuf=buf(2, 3, h, kf), ycol=wide(2, h, LANES), zbuf=buf(3, kf, kf),
        own_legs=buf(3, 2, h, half), other=buf(3, 2, h, CHUNK), prods=buf(2, 2, h, half),
        zero=wide(h, LANES), wbuf=buf(2 * h, kf),
        part=buf(2, 2, *block), mate_in=buf(2, *block), chip=buf(2, *block),
        a_field=buf(2, fields, *a_block), b_far=buf(2, far, *b_block), mid=buf(2, *block),
        a_far=buf(2, far, *a_block), b_field=buf(2, fields, *b_block), fin=buf(2, 2, *block),
        load_sem=dma(12), sbf=dma(far), rbf=dma(far), sbm=dma(nrows // 2), rbm=dma(nrows // 2),
        sf1=dma(2), rf1=dma(2), sf2=dma(2, far), rf2=dma(2, far), sf3=dma(2), rf3=dma(2),
        sz=dma(nreal - 1), rz=dma(nreal - 1), sp=dma(nrows - 1), rp=dma(nrows - 1),
        s1=dma(2), r1=dma(2), saf=dma(2, fields), raf=dma(2, fields),
        sbfield=dma(2, fields), rbfield=dma(2, fields),
        say=dma(2, far), ray=dma(2, far), sby=dma(2, far), rby=dma(2, far), s3=dma(2), r3=dma(2),
    )
    hbm = pl.BlockSpec(memory_space=pl.ANY)
    vmem = pl.BlockSpec(memory_space=pltpu.VMEM)
    smem = pl.BlockSpec(memory_space=pltpu.SMEM)
    tables = [t["fy"], t["cs"], rows, pick_cols, t["ty"], t["ft"], t["fx"], t["ts"], pick, turn]
    return pl.pallas_call(
        functools.partial(kernel, (nrows, nreal, nfield, t["unit"], t["step"]), tuple(scratch)),
        out_shape=[
            jax.ShapeDtypeStruct((2, 2, kf, cols), F32),
            jax.ShapeDtypeStruct((kf, cols), F32),
        ],
        in_specs=[hbm] * 2 + [vmem] * 5 + [smem] + [hbm] * len(tables),
        out_specs=[vmem] * 2,
        scratch_shapes=list(scratch.values()),
        compiler_params=pltpu.CompilerParams(
            collective_id=0, has_side_effects=True, vmem_limit_bytes=VMEM_LIMIT
        ),
        cost_estimate=pl.CostEstimate(
            flops=32 * h * npix * kf, bytes_accessed=24 * 2**20, transcendentals=0
        ),
    )(sims, data, mask_flags, bins, signal, noise, norm, matching, *(jnp.asarray(v) for v in tables))


def body(nrows, nreal, nfield, sims, data, mask_flags, bins, cl_signal, cl_noise, norm, matching):
    out, ncell = estimates(
        sims[0, 0], data[0], mask_flags, bins, cl_signal, cl_noise, norm[None], matching,
        nrows, nreal, nfield,
    )
    return (out * ncell)[None]


def solution(mesh):
    in_specs = (
        P("real", "field", "rows", None),
        P("field", "rows", None),
        P("rows", None),
        P(None, "rows"),
        P("field", None),
        P("field", None),
        P(),
        P(),
    )
    out_specs = P("real", None, None, None, "rows")
    f = functools.partial(body, mesh.shape["rows"], mesh.shape["real"], mesh.shape["field"])
    return jax.shard_map(f, mesh=mesh, in_specs=in_specs, out_specs=out_specs, check_vma=False)
```

```python
import functools
import math
import types

import jax
import jax.numpy as jnp
import numpy as np
from jax import lax
from jax.experimental import pallas as pl
from jax.experimental.pallas import tpu as pltpu
from jax.sharding import PartitionSpec as P

TILE = 128
LANES = 128
TAIL = 16
CHUNK = 256
BF = jnp.bfloat16
F32 = jnp.float32
VMEM_LIMIT = 60 * 1024 * 1024
MESH = pl.DeviceIdType.MESH
NT = (((1,), (1,)), ((), ()))


def round_bf(values):
    return np.asarray(values, np.float32).astype(BF)


@functools.lru_cache
def constants(npix, kf, nrows):
    top, half, h = kf // 2, npix // 2, npix // nrows
    scale, step = npix ** -0.5, 2.0 * math.pi / npix

    def cis(pixels, freqs):
        angle = np.mod(pixels[:, None] * freqs[None, :], npix) * step
        rounded = [round_bf(f(angle) * scale).astype(np.float32) for f in (np.cos, np.sin)]
        return rounded

    x, y = np.arange(half), np.arange(npix)
    fy, fx = [], []
    for kx in (np.arange(2, top + 1, 2), np.arange(1, top, 2)):
        c, s = cis(x, kx)
        lx = kx * step
        fy.append(np.concatenate([c, -s], axis=1))
        fx.append(np.concatenate([lx * s, lx * c], axis=1))
    fy, fx = np.stack(fy), np.stack(fx)
    ky = np.arange(1, top + 1)
    c, s = (v.T for v in cis(y, ky))
    ly = (ky * step)[:, None]
    zero = np.full((1, npix), round_bf(scale).astype(np.float32))
    pad = np.zeros((TAIL - 1, npix), np.float32)
    split = lambda a: a.reshape(a.shape[0], nrows, h).transpose(1, 0, 2)
    cs = split(np.concatenate([c, s, zero, pad]))
    sy = split(np.concatenate([ly * s, -ly * c, 0 * zero, pad]))
    return dict(
        fy=round_bf(fy),
        fx=round_bf(fx),
        ft=round_bf(fy.transpose(0, 2, 1)),
        cs=round_bf(cs),
        ty=round_bf(cs[:, : 2 * top].transpose(0, 2, 1)),
        ts=round_bf(np.concatenate([cs, sy], axis=2)),
        unit=float(round_bf(scale)),
        step=step,
    )


def lane_of(k, top):
    return k // 2 - 1 if k % 2 == 0 else top // 2 + (k - 1) // 2


@functools.lru_cache
def cell_tables(kf):
    top = kf // 2
    rows = np.zeros((kf + TAIL, kf), np.float32)
    cols = np.zeros((kf, kf), np.float32)
    for k in range(1, top + 1):
        if k < top:
            rows[k - 1, top + k] = 1.0
            cols[top + k, lane_of(k, top)] = 1.0
        rows[top + k - 1, top - k] = 1.0
        cols[top - k, top + lane_of(k, top)] = 1.0
    rows[kf, top] = 1.0
    return round_bf(rows), round_bf(cols)


@functools.lru_cache
def output_tables(kf, nrows):
    top, cols = kf // 2, kf // nrows
    pick = np.zeros((nrows, kf, 2 * LANES), np.float32)
    for r in range(nrows):
        for j in range(cols):
            kx = r * cols + j - top
            if kx == 0:
                continue
            lane = lane_of(abs(kx), top)
            lane = lane % (top // 2) + (lane // (top // 2)) * top
            pick[r, lane, j] = 1.0
            pick[r, lane + top // 2, LANES + j] = 1.0 if kx > 0 else -1.0
    turn = np.zeros((2, top, top), np.float32)
    for i in range(top):
        turn[0, i, top - 1 - i] = 1.0
        if i:
            turn[1, i, i - 1] = 1.0
    return round_bf(pick), round_bf(turn)


def send(src, dst, sems, at, device):
    copy = pltpu.make_async_remote_copy(
        src_ref=src,
        dst_ref=dst,
        send_sem=sems[0].at[at],
        recv_sem=sems[1].at[at],
        device_id=device,
        device_id_type=MESH,
    )
    copy.start()
    return copy


def greet(devices):
    barrier = pltpu.get_barrier_semaphore()
    for device in devices:
        pl.semaphore_signal(barrier, inc=1, device_id=device, device_id_type=MESH)
    return lambda: pl.semaphore_wait(barrier, len(devices))


def row_places(nrows):
    r = lax.axis_index("rows")
    core = lax.rem(r, 2)
    mate = {"rows": r + 1 - 2 * core}
    others = [{"rows": lax.rem(r + 2 * d, nrows)} for d in range(1, nrows // 2)]
    return r, core, mate, others


def expanded(flags):
    rows, tiles = flags.shape
    return jnp.concatenate(
        [jnp.broadcast_to(flags[:, j : j + 1], (rows, TILE)) for j in range(tiles)], axis=1
    )


def transposed_line(columns):
    return jnp.sum(columns.T, axis=0, keepdims=True)


def as_tail(*rows):
    shape = (TAIL, rows[0].shape[1])
    row = lax.broadcasted_iota(jnp.int32, shape, 0)
    tail = jnp.zeros(shape, F32)
    for i, v in enumerate(rows):
        tail = jnp.where(row == i, jnp.broadcast_to(v, shape), tail)
    return tail


def store_blocks(part, sums, tail):
    blocks = part.shape[0]
    share = sums.shape[0] // blocks
    for b in range(blocks):
        part[b, :share] = sums[b * share : (b + 1) * share].astype(BF)
        part[b, share:] = tail.astype(BF)


def lane_sums(values):
    total = values[:, :LANES]
    for i in range(LANES, values.shape[1], LANES):
        total = total + values[:, i : i + LANES]
    return total


def kernel(
    sizes, names,
    sims_ref, data_ref, mask_ref, bins_ref, signal_ref, noise_ref, norm_ref, matching_ref,
    fy_ref, cs_ref, rows_ref, cols_ref, ty_ref, ft_ref, fx_ref, ts_ref, pick_ref, turn_ref,
    out_ref,
    *scratch,
):
    nrows, nreal, nfield, unit, step = sizes
    s = types.SimpleNamespace(**dict(zip(names, scratch)))
    h, kf = s.ty.shape
    top, quarter, half = kf // 2, kf // 4, s.even.shape[1]
    cols = bins_ref.shape[1]
    nbins = norm_ref.shape[1]
    r, core, mate, others = row_places(nrows)
    y, chips = r // 2, nrows // 2
    real = lax.axis_index("real")
    field = lax.axis_index("field")
    along_real = [{"real": lax.rem(real + d, nreal)} for d in range(1, nreal)]
    along_field = [{"field": lax.rem(field + d, nfield)} for d in range(1, nfield)]
    share = top // chips

    block_of = core * chips + y
    from_chip = [core * chips + lax.rem(y - d + chips, chips) for d in range(chips)]

    copies = {}
    tiles = h // TILE
    for m, src in enumerate((sims_ref, data_ref)):
        for t in range(tiles):
            rows = pl.ds(t * TILE, TILE)
            copies[m, t] = pltpu.make_async_copy(
                src.at[rows], s.maps.at[m, rows], s.map_sem.at[m, t]
            )
    for i, (name, src, dst) in enumerate(
        [("fy", fy_ref, s.fy), ("cs", cs_ref.at[r], s.cs), ("rows", rows_ref, s.rows),
         ("cols", cols_ref, s.cols), ("ty", ty_ref.at[r], s.ty), ("ft", ft_ref, s.ft),
         ("fx", fx_ref, s.fx), ("ts", ts_ref.at[r], s.ts), ("pick", pick_ref.at[r], s.pick),
         ("turn", turn_ref, s.turn)]
    ):
        copies[name] = pltpu.make_async_copy(src, dst, s.load_sem.at[i])

    def load(*which):
        for name in which:
            copies[name].start()

    def loaded(*which):
        for name in which:
            copies[name].wait()

    load(*((0, t) for t in range(tiles)), "fy", "cs")
    arrived = greet(along_real + [mate] + others + along_field)


    def bins_out():
        s.bins[r] = bins_ref[...].astype(F32).astype(BF)
        return [
            send(s.bins.at[r], s.bins.at[r], (s.sbf, s.rbf), d, device)
            for d, device in enumerate(others)
        ]

    def bins_on(copies):
        for copy in copies:
            copy.wait()
        blocks = [lax.rem(r + 2 * d, nrows) for d in range(chips)]
        return [
            send(s.bins.at[block], s.bins.at[block], (s.sbm, s.rbm), d, mate)
            for d, block in enumerate(blocks)
        ]

    def take(t, idx):
        table = jnp.broadcast_to(s.tab[t : t + 1, :], (idx.shape[0], LANES))
        parts = [
            jnp.take_along_axis(table[:, : idx.shape[1]] if idx.shape[1] < LANES else table,
                                idx[:, i : i + LANES], axis=1, mode="promise_in_bounds")
            for i in range(0, idx.shape[1], LANES)
        ]
        return parts[0] if len(parts) == 1 else jnp.concatenate(parts, axis=1)

    def filter_cells():
        weight = 1.0 / (signal_ref[...] + noise_ref[...])
        s.tab[...] = jnp.zeros_like(s.tab)
        s.tab[0:1, :nbins] = 4.0 * weight
        s.tab[1:2, :nbins] = 4.0 * (signal_ref[...] * weight)
        s.tab[2:3, :nbins] = 2.0 * norm_ref[...]
        s.ncell[...] = take(2, bins_ref[...])
        by_row = [
            jnp.dot(s.rows[...], s.bins[i], preferred_element_type=F32).astype(BF) for i in range(nrows)
        ]
        by_row = jnp.concatenate(by_row, axis=1)
        cells = jnp.dot(by_row, s.cols[...], preferred_element_type=F32)
        row = lax.broadcasted_iota(jnp.int32, cells.shape, 0)
        lane = lax.broadcasted_iota(jnp.int32, cells.shape, 1)
        absent = (row == top - 1) | (lane == quarter - 1)
        s.idx[...] = jnp.where(absent, nbins, cells.astype(jnp.int32))
        s.by_row[...] = by_row

    def filters(t):
        shape = (top, top)
        ky = lax.broadcasted_iota(jnp.int32, shape, 0) + 1
        at = lax.broadcasted_iota(jnp.int32, shape, 1)
        kx = jnp.where(at < quarter, 2 * at + 2, 2 * (at - quarter) + 1)
        ly, lx = ky.astype(F32) * step, kx.astype(F32) * step
        v = take(t, s.idx[...])
        pp, pm = v[:top, :top], v[:top, top:]
        mp, mm = v[top:kf, :top], v[top:kf, top:]
        a, b = (pp + mm) + (mp + pm), (pp + mm) - (mp + pm)
        zero_row = (v[kf : kf + 1, :top] + v[kf : kf + 1, top:]) * unit
        hot = (lax.broadcasted_iota(jnp.int32, (TAIL, kf), 1) == top).astype(F32).astype(BF)
        line = lax.dot_general(hot, s.by_row[:kf], NT, preferred_element_type=F32)
        lane = lax.broadcasted_iota(jnp.int32, (TAIL, kf), 1)
        line = take(t, jnp.where(lane == top - 1, nbins, line.astype(jnp.int32)))[:1]
        line = line[:, :top] + line[:, top:]
        if t == 0:
            s.tabs[0] = a
            s.tabs[1] = b
            dc = take(0, s.by_row[kf:, top : top + LANES].astype(F32).astype(jnp.int32))[:1]
            dc = jnp.where(lax.broadcasted_iota(jnp.int32, dc.shape, 1) == 0, dc * unit, 0.0)
            s.lines[0:1, :top] = zero_row
            s.lines[1:2, :] = jnp.concatenate([line, line], axis=1)
            s.lines[3:4, :LANES] = dc
        else:
            s.tabs[2] = lx * a
            s.tabs[3] = lx * b
            s.tabs[4] = ly * a
            s.tabs[5] = ly * b
            ly_row = (lax.broadcasted_iota(jnp.int32, (1, top), 1) + 1).astype(F32) * step
            s.lines[0:1, top:] = zero_row * lx[:1]
            s.lines[2:3, :] = jnp.concatenate([ly_row * line, -(ly_row * line)], axis=1)


    def fold(m):
        for t in range(tiles):
            loaded((m, t))
            rows = pl.ds(t * TILE, TILE)
            flags = s.mask[t]
            lo = s.maps[m, rows, :half].astype(F32) * flags[:, :half]
            hi = s.maps[m, rows, half:].astype(F32) * flags[:, half:]
            both = lo + hi
            s.even[rows, :] = both.astype(BF)
            s.odd[rows, :] = (lo - hi).astype(BF)
            s.zero_b[rows, :] = (lane_sums(both) * unit).astype(BF)

    def columns(m, q):
        side = s.odd if q else s.even
        out = jnp.dot(side[...], s.fy[q], preferred_element_type=F32)
        s.cells[...] = out.astype(BF)
        sums = jnp.dot(s.cs[...], s.cells[...], preferred_element_type=F32)
        rows = [sums[kf : kf + 1]]
        if q == 0:
            line = jnp.dot(s.cs[...], s.zero_b[...], preferred_element_type=F32)
            turned = transposed_line(line[:kf])
            corner = jnp.concatenate([line[kf : kf + 1], jnp.zeros((1, top - LANES), F32)], axis=1)
            rows += [turned[:, :top], corner, turned[:, top:]]
        store_blocks(s.fpart.at[m, q], sums[:kf], as_tail(*rows))
        return send(
            s.fpart.at[m, q, half_of(1 - core)], s.fmate.at[m, q], (s.sf1, s.rf1), (m, q), mate
        )

    half_of = lambda c: pl.ds(c * chips, chips)

    def cells_to_chips(m, q, first):
        first.wait()
        s.fchip[m, q] = (s.fpart[m, q, half_of(core)].astype(F32) + s.fmate[m, q].astype(F32)).astype(BF)
        return [
            send(s.fchip.at[m, q, lax.rem(y + d + 1, chips)], s.ffar.at[m, q, d], (s.sf2, s.rf2), (m, q, d), device)
            for d, device in enumerate(others)
        ]

    def cells_done(m, q, copies):
        total = s.fchip[m, q, y].astype(F32)
        for d, copy in enumerate(copies):
            copy.wait()
            total = total + s.ffar[m, q, d].astype(F32)
        s.pq[m, q, block_of] = total.astype(BF)
        return gather_out(m, q)


    def gather_out(m, q):
        sends = lambda sems, at, device: send(
            s.pq.at[m, q, block_of], s.pq.at[m, q, block_of], sems, (m, q, at), device
        )
        far = [sends((s.sgf, s.rgf), d, device) for d, device in enumerate(others)]
        return far, [sends((s.sgm, s.rgm), 0, mate)]

    def gather_on(m, q, copies):
        far, near = copies
        for d, copy in enumerate(far):
            copy.wait()
            block = from_chip[d + 1]
            near.append(
                send(s.pq.at[m, q, block], s.pq.at[m, q, block], (s.sgm, s.rgm), (m, q, d + 1), mate)
            )
        return near

    def finish(copies):
        for copy in copies:
            copy.wait()


    def partner_out(q):
        return [
            send(s.pq.at[0, q, block_of], s.zin.at[q, d], (s.sz, s.rz), (q, d), device)
            for d, device in enumerate(along_real)
        ]

    def partner_on(q, copies):
        partner = matching_ref[real]
        named = lambda d: jnp.where(lax.rem(real - d + nreal, nreal) == partner, 1.0, 0.0)
        total = named(0) * s.pq[0, q, block_of].astype(F32)
        for d, copy in enumerate(copies):
            copy.wait()
            total = total + named(d + 1) * s.zin[q, d].astype(F32)
        s.pq[2, q, block_of] = total.astype(BF)
        return gather_out(2, q)

    def make_y(m, q, slot):
        tail = s.pq[m, q, 0, share:].astype(F32)
        at = slice(q * quarter, (q + 1) * quarter)
        for b in range(chips):
            rows = slice(b * share, (b + 1) * share)
            p_re, p_im, q_re, q_im = (
                s.pq[m, q, c * chips + b, :share, i * quarter : (i + 1) * quarter].astype(F32)
                for c in range(2)
                for i in range(2)
            )
            aw, bw, xa, xb, ya, yb = (s.tabs[i, rows, at] for i in range(6))
            sets = (
                (aw * p_re + bw * q_im, aw * p_im - bw * q_re, aw * q_re - bw * p_im, aw * q_im + bw * p_re),
                (xb * q_re - xa * p_im, xb * q_im + xa * p_re, -(xb * p_re) - xa * q_im, xa * q_re - xb * p_im),
                (ya * q_re - yb * p_im, ya * q_im + yb * p_re, -(ya * p_re) - yb * q_im, yb * q_re - ya * p_im),
            )
            for leg, values in enumerate(sets):
                for i, v in enumerate(values):
                    where = (i % 2) * quarter
                    row = (i // 2) * top + b * share
                    s.zbuf[leg, row : row + share, where : where + quarter] = v.astype(BF)
        w_row = s.lines[0:1, q * quarter : (q + 1) * quarter]
        g_row = s.lines[0:1, top + q * quarter : top + (q + 1) * quarter]
        re, im = tail[0:1, :quarter], tail[0:1, quarter:]
        zero_rows = (
            jnp.concatenate([w_row * re, w_row * im], axis=1),
            jnp.concatenate([-(g_row * im), g_row * re], axis=1),
            None,
        )
        for leg in range(3):
            out = jnp.dot(s.ty[...], s.zbuf[leg], preferred_element_type=F32)
            if zero_rows[leg] is not None:
                out = out + zero_rows[leg]
            s.ybuf[slot, q, leg] = out.astype(BF)
        if q == 0:
            b_line = s.lines[1:2, :] * jnp.concatenate([tail[1:2], tail[3:4]], axis=1)
            y_line = s.lines[2:3, :] * jnp.concatenate([tail[3:4], tail[1:2]], axis=1)
            row = lax.broadcasted_iota(jnp.int32, (LANES, kf), 0)
            both = jnp.where(row == 0, b_line, jnp.where(row == 1, y_line, 0.0)).astype(BF)
            col = lax.dot_general(s.ty[...], both, NT, preferred_element_type=F32)
            dc = jnp.sum(tail[2:3, :LANES], axis=1, keepdims=True) * s.lines[3:4, :LANES]
            s.ycol[slot] = (col + dc) * unit

    def legs_done(slot, q):
        dest = s.other if slot else s.own_legs
        for leg in range(3):
            for here in (slice(at, at + CHUNK) for at in range(0, half, CHUNK)):
                out = jnp.dot(s.ybuf[slot, q, leg], s.ft[q, :, here], preferred_element_type=F32)
                if q == 0 and leg != 1:
                    lane = 0 if leg == 0 else 1
                    out = out + s.ycol[slot, :, lane : lane + 1]
                dest[leg, q, :, here] = out.astype(BF)

    def products():
        rows_of = 16

        @pl.loop(0, h // rows_of)
        def _(c):
            rows = pl.ds(pl.multiple_of(c * rows_of, rows_of), rows_of)
            total = jnp.zeros((rows_of, LANES), F32)
            for here in (slice(at, at + CHUNK) for at in range(0, half, CHUNK)):
                o = [[s.own_legs[leg, q, rows, here] for q in range(2)] for leg in range(3)]
                t = [[s.other[leg, q, rows, here] for q in range(2)] for leg in range(3)]
                for i, leg in enumerate((1, 2)):
                    for q in range(2):
                        out = (t[leg][0] * o[0][q] + t[leg][1] * o[0][1 - q]) + (
                            o[leg][0] * t[0][q] + o[leg][1] * t[0][1 - q]
                        )
                        s.prods[i, q, rows, here] = out
                        if q == 0 and i == 1:
                            total = total + lane_sums(out.astype(F32))
            s.zero[rows, :] = total

    def pair_cells(e):
        q = e % 2
        for i, table in enumerate((s.fx, s.fy)):
            out = jnp.dot(s.prods[i, q], table[q], preferred_element_type=F32)
            s.wbuf[q, i * h : (i + 1) * h, :] = out.astype(BF)

    def pair_sums(e):
        q = e % 2
        sums = jnp.dot(s.ts[...], s.wbuf[q], preferred_element_type=F32)
        rows = [sums[kf : kf + 1]]
        if q == 1:
            column = (s.zero[...] * unit).astype(BF)
            line = transposed_line(jnp.dot(s.ts[:kf, h:], column, preferred_element_type=F32))
            rows += [line[:, :top], line[:, top:]]
        store_blocks(s.part.at[e], sums[:kf], as_tail(*rows))

    a_rows, b_rows = pl.ds(0, top // 2), pl.ds(top // 2, top // 2 + TAIL)

    def to_mate(e):
        return send(s.part.at[e, 1 - core], s.mate_in.at[e], (s.s1, s.r1), e, mate)

    def first_out(e, copy):
        copy.wait()
        s.chip[e] = (s.part[e, core].astype(F32) + s.mate_in[e].astype(F32)).astype(BF)
        a = [
            send(s.chip.at[e, a_rows], s.a_field.at[e, d], (s.saf, s.raf), (e, d), device)
            for d, device in enumerate(along_field)
        ]
        b = [
            send(s.chip.at[e, b_rows], s.b_far.at[e, d], (s.sby, s.rby), (e, d), device)
            for d, device in enumerate(others)
        ]
        return a, b

    def gathered(total, copies, slots):
        total = total.astype(F32)
        for d, copy in enumerate(copies):
            copy.wait()
            total = total + slots(d).astype(F32)
        return total.astype(BF)

    def second_out(e, copies):
        a, b = copies
        s.mid[e, a_rows] = gathered(s.chip[e, a_rows], a, lambda d: s.a_field[e, d])
        a = [
            send(s.mid.at[e, a_rows], s.a_far.at[e, d], (s.say, s.ray), (e, d), device)
            for d, device in enumerate(others)
        ]
        s.mid[e, b_rows] = gathered(s.chip[e, b_rows], b, lambda d: s.b_far[e, d])
        b = [
            send(s.mid.at[e, b_rows], s.b_field.at[e, d], (s.sbfield, s.rbfield), (e, d), device)
            for d, device in enumerate(along_field)
        ]
        return a, b

    def last_out(e, copies):
        a, b = copies
        s.fin[e, core, a_rows] = gathered(s.mid[e, a_rows], a, lambda d: s.a_far[e, d])
        s.fin[e, core, b_rows] = gathered(s.mid[e, b_rows], b, lambda d: s.b_field[e, d])
        return send(s.fin.at[e, core], s.fin.at[e, core], (s.s3, s.r3), e, mate)

    def each(step, pair, state=None):
        return [
            step(2 * pair + q) if state is None else step(2 * pair + q, state[q]) for q in range(2)
        ]

    def assemble(pair, copies):
        picked = [0.0, 0.0, 0.0]
        for q in range(2):
            e = 2 * pair + q
            copies[q].wait()
            tail = s.fin[e, 0, top:]
            if q == 1:
                lines = [tail.astype(F32)[1:2], tail.astype(F32)[2:3]]
            for i, v in enumerate((s.fin[e, 0, :top], s.fin[e, 1, :top], tail)):
                chosen = s.pick[q * top : (q + 1) * top, :]
                picked[i] = picked[i] + jnp.dot(v, chosen, preferred_element_type=F32)
        zero_line = picked[2][:1]
        column = jnp.broadcast_to(jnp.concatenate(lines, axis=1), (LANES, kf)).T
        lane = lax.broadcasted_iota(jnp.int32, (kf, LANES), 1)
        column = jnp.where(lane + r * cols == top, column, 0.0)
        p_re, p_im = picked[0][:, :LANES] + column[:top], picked[0][:, LANES:]
        q_re, q_im = picked[1][:, :LANES] + column[top:], picked[1][:, LANES:]
        plus = jnp.concatenate([p_re + q_im, p_im - q_re], axis=1).astype(BF)
        minus = jnp.concatenate([p_re - q_im, p_im + q_re], axis=1).astype(BF)
        lower = jnp.dot(s.turn[0], minus, preferred_element_type=F32)
        upper = jnp.dot(s.turn[1], plus, preferred_element_type=F32)
        row = lax.broadcasted_iota(jnp.int32, upper.shape, 0)
        upper = jnp.where(row == 0, zero_line, upper)
        for i in range(2):
            at = slice(i * LANES, i * LANES + cols)
            out_ref[pair, i, :top] = (lower[:, at] * s.ncell[:top]).astype(BF)
            out_ref[pair, i, top:] = (upper[:, at] * s.ncell[top:]).astype(BF)

    full = expanded(mask_ref[...].astype(F32))
    for t in range(full.shape[0]):
        s.mask[t] = full[t : t + 1]
    fold(0)
    arrived()
    bins = bins_out()
    load(*((1, t) for t in range(tiles)), "rows", "cols")
    loaded("fy", "cs")
    own, data = [columns(0, 0)], []
    own.append(columns(0, 1))
    fold(1)
    load("ty", "ft", "fx", "ts", "pick", "turn")
    own[0] = cells_to_chips(0, 0, own[0])
    data.append(columns(1, 0))
    own[1] = cells_to_chips(0, 1, own[1])
    bins = bins_on(bins)
    data.append(columns(1, 1))
    loaded("rows", "cols")
    own[0] = cells_done(0, 0, own[0])
    finish(bins)
    filter_cells()
    own[1] = cells_done(0, 1, own[1])
    partner = [partner_out(0)]
    data[0] = cells_to_chips(1, 0, data[0])
    filters(0)
    partner.append(partner_out(1))
    data[1] = cells_to_chips(1, 1, data[1])
    filters(1)
    own[0] = gather_on(0, 0, own[0])
    loaded("ty", "ft")
    own[1] = gather_on(0, 1, own[1])
    finish(own[0])
    make_y(0, 0, 0)
    data[0] = cells_done(1, 0, data[0])
    legs_done(0, 0)
    data[1] = cells_done(1, 1, data[1])
    finish(own[1])
    make_y(0, 1, 0)
    data[0] = gather_on(1, 0, data[0])
    legs_done(0, 1)
    data[1] = gather_on(1, 1, data[1])
    finish(data[0])
    make_y(1, 0, 1)
    legs_done(1, 0)
    partner[0] = partner_on(0, partner[0])
    finish(data[1])
    make_y(1, 1, 1)
    legs_done(1, 1)
    partner[1] = partner_on(1, partner[1])
    products()
    partner[0] = gather_on(2, 0, partner[0])
    loaded("fx", "ts", "pick", "turn")
    pair_cells(0)
    pair_sums(0)
    ds = [to_mate(0)]
    partner[1] = gather_on(2, 1, partner[1])
    pair_cells(1)
    pair_sums(1)
    ds.append(to_mate(1))
    finish(partner[0])
    make_y(2, 0, 1)
    ds[0] = first_out(0, ds[0])
    legs_done(1, 0)
    ds[1] = first_out(1, ds[1])
    finish(partner[1])
    make_y(2, 1, 1)
    legs_done(1, 1)
    ds[0] = second_out(0, ds[0])
    products()
    ds[1] = second_out(1, ds[1])
    pair_cells(2)
    pair_sums(2)
    ss = [to_mate(2)]
    pair_cells(3)
    ss[0] = first_out(2, ss[0])
    pair_sums(3)
    ss.append(to_mate(3))
    ds = each(last_out, 0, ds)
    ss[1] = first_out(3, ss[1])
    ss[0] = second_out(2, ss[0])
    assemble(0, ds)
    ss[1] = second_out(3, ss[1])
    ss = each(last_out, 1, ss)
    assemble(1, ss)


def estimates(sims, data, mask_flags, bins, signal, noise, norm, matching, nrows, nreal, nfield):
    h, npix = sims.shape
    kf, cols = bins.shape
    top, half = kf // 2, npix // 2
    t = constants(npix, kf, nrows)
    rows, pick_cols = cell_tables(kf)
    pick, turn = output_tables(kf, nrows)
    far, fields = max(nrows // 2 - 1, 1), max(nfield - 1, 1)
    chips = nrows // 2
    share = top // chips
    piece, block = (share + TAIL, top), (top + TAIL, top)
    a_block, b_block = (top // 2, top), (top // 2 + TAIL, top)
    buf = lambda *shape: pltpu.VMEM(shape, BF)
    wide = lambda *shape: pltpu.VMEM(shape, F32)
    dma = lambda *shape: pltpu.SemaphoreType.DMA(shape)
    scratch = dict(
        maps=buf(2, h, npix), fy=buf(2, half, top), cs=buf(kf + TAIL, h), rows=buf(kf + TAIL, kf),
        cols=buf(kf, kf), ty=buf(h, kf), ft=buf(2, top, half), fx=buf(2, half, top),
        ts=buf(kf + TAIL, 2 * h), pick=buf(kf, 2 * LANES), turn=buf(2, top, top),
        idx=pltpu.VMEM((kf + TAIL, kf), jnp.int32), by_row=buf(kf + TAIL, kf),
        mask=wide(h // TILE, 1, npix), bins=buf(nrows, kf, cols), tab=wide(8, LANES),
        tabs=wide(6, top, top), lines=wide(8, kf),
        even=buf(h, half), odd=buf(h, half), zero_b=buf(h, LANES), cells=buf(h, top),
        fpart=buf(2, 2, nrows, *piece), fmate=buf(2, 2, chips, *piece), fchip=buf(2, 2, chips, *piece),
        ffar=buf(2, 2, far, *piece), pq=buf(3, 2, nrows, *piece), zin=buf(2, nreal - 1, *piece),
        ybuf=buf(2, 2, 3, h, top), ycol=wide(2, h, LANES), zbuf=buf(3, kf, top),
        own_legs=buf(3, 2, h, half), other=buf(3, 2, h, half), prods=buf(2, 2, h, half),
        zero=wide(h, LANES), wbuf=buf(2, 2 * h, top), ncell=wide(kf, cols),
        part=buf(4, 2, *block), mate_in=buf(4, *block), chip=buf(4, *block),
        a_field=buf(4, fields, *a_block), b_far=buf(4, far, *b_block), mid=buf(4, *block),
        a_far=buf(4, far, *a_block), b_field=buf(4, fields, *b_block), fin=buf(4, 2, *block),
        load_sem=dma(10), map_sem=dma(2, h // TILE), sbf=dma(far), rbf=dma(far), sbm=dma(chips), rbm=dma(chips),
        sf1=dma(2, 2), rf1=dma(2, 2), sf2=dma(2, 2, far), rf2=dma(2, 2, far),
        sgf=dma(3, 2, far), rgf=dma(3, 2, far), sgm=dma(3, 2, chips), rgm=dma(3, 2, chips),
        sz=dma(2, nreal - 1), rz=dma(2, nreal - 1),
        s1=dma(4), r1=dma(4), saf=dma(4, fields), raf=dma(4, fields),
        sbfield=dma(4, fields), rbfield=dma(4, fields),
        say=dma(4, far), ray=dma(4, far), sby=dma(4, far), rby=dma(4, far), s3=dma(4), r3=dma(4),
    )
    hbm = pl.BlockSpec(memory_space=pl.ANY)
    vmem = pl.BlockSpec(memory_space=pltpu.VMEM)
    smem = pl.BlockSpec(memory_space=pltpu.SMEM)
    tables = [t["fy"], t["cs"], rows, pick_cols, t["ty"], t["ft"], t["fx"], t["ts"], pick, turn]
    return pl.pallas_call(
        functools.partial(kernel, (nrows, nreal, nfield, t["unit"], t["step"]), tuple(scratch)),
        out_shape=jax.ShapeDtypeStruct((2, 2, kf, cols), BF),
        in_specs=[hbm] * 2 + [vmem] * 5 + [smem] + [hbm] * len(tables),
        out_specs=vmem,
        scratch_shapes=list(scratch.values()),
        compiler_params=pltpu.CompilerParams(
            collective_id=0, has_side_effects=True, vmem_limit_bytes=VMEM_LIMIT
        ),
        cost_estimate=pl.CostEstimate(
            flops=32 * h * npix * kf, bytes_accessed=24 * 2**20, transcendentals=0
        ),
    )(sims, data, mask_flags, bins, signal, noise, norm, matching, *(jnp.asarray(v) for v in tables))


def body(nrows, nreal, nfield, sims, data, mask_flags, bins, cl_signal, cl_noise, norm, matching):
    out = estimates(
        sims[0, 0], data[0], mask_flags, bins, cl_signal, cl_noise, norm[None], matching,
        nrows, nreal, nfield,
    )
    return out.astype(F32)[None]


def solution(mesh):
    in_specs = (
        P("real", "field", "rows", None),
        P("field", "rows", None),
        P("rows", None),
        P(None, "rows"),
        P("field", None),
        P("field", None),
        P(),
        P(),
    )
    out_specs = P("real", None, None, None, "rows")
    f = functools.partial(body, mesh.shape["rows"], mesh.shape["real"], mesh.shape["field"])
    return jax.shard_map(f, mesh=mesh, in_specs=in_specs, out_specs=out_specs, check_vma=False)
```

```python
import functools
import math
import types

import jax
import jax.numpy as jnp
import numpy as np
from jax import lax
from jax.experimental import pallas as pl
from jax.experimental.pallas import tpu as pltpu
from jax.sharding import PartitionSpec as P

TILE = 128
LANES = 128
TAIL = 16
CHUNK = 256
BF = jnp.bfloat16
F32 = jnp.float32
VMEM_LIMIT = 60 * 1024 * 1024
MESH = pl.DeviceIdType.MESH
NT = (((1,), (1,)), ((), ()))


def round_bf(values):
    return np.asarray(values, np.float32).astype(BF)


@functools.lru_cache
def constants(npix, kf, nrows):
    top, half, h = kf // 2, npix // 2, npix // nrows
    scale, step = npix ** -0.5, 2.0 * math.pi / npix

    def cis(pixels, freqs):
        angle = np.mod(pixels[:, None] * freqs[None, :], npix) * step
        rounded = [round_bf(f(angle) * scale).astype(np.float32) for f in (np.cos, np.sin)]
        return rounded

    x, y = np.arange(half), np.arange(npix)
    fy, fx = [], []
    for kx in (np.arange(2, top + 1, 2), np.arange(1, top, 2)):
        c, s = cis(x, kx)
        lx = kx * step
        fy.append(np.concatenate([c, -s], axis=1))
        fx.append(np.concatenate([lx * s, lx * c], axis=1))
    fy, fx = np.stack(fy), np.stack(fx)
    ky = np.arange(1, top + 1)
    c, s = (v.T for v in cis(y, ky))
    ly = (ky * step)[:, None]
    zero = np.full((1, npix), round_bf(scale).astype(np.float32))
    pad = np.zeros((TAIL - 1, npix), np.float32)
    split = lambda a: a.reshape(a.shape[0], nrows, h).transpose(1, 0, 2)
    cs = split(np.concatenate([c, s, zero, pad]))
    sy = split(np.concatenate([ly * s, -ly * c, 0 * zero, pad]))
    return dict(
        fy=round_bf(fy),
        fx=round_bf(fx),
        ft=round_bf(fy.transpose(0, 2, 1)),
        cs=round_bf(cs),
        ty=round_bf(cs[:, : 2 * top].transpose(0, 2, 1)),
        ts=round_bf(np.concatenate([cs, sy], axis=2)),
        unit=float(round_bf(scale)),
        step=step,
    )


def lane_of(k, top):
    return k // 2 - 1 if k % 2 == 0 else top // 2 + (k - 1) // 2


@functools.lru_cache
def cell_tables(kf):
    top = kf // 2
    rows = np.zeros((kf + TAIL, kf), np.float32)
    cols = np.zeros((kf, kf), np.float32)
    for k in range(1, top + 1):
        if k < top:
            rows[k - 1, top + k] = 1.0
            cols[top + k, lane_of(k, top)] = 1.0
        rows[top + k - 1, top - k] = 1.0
        cols[top - k, top + lane_of(k, top)] = 1.0
    rows[kf, top] = 1.0
    return round_bf(rows), round_bf(cols)


@functools.lru_cache
def output_tables(kf, nrows):
    top, cols = kf // 2, kf // nrows
    pick = np.zeros((nrows, kf, 2 * LANES), np.float32)
    for r in range(nrows):
        for j in range(cols):
            kx = r * cols + j - top
            if kx == 0:
                continue
            lane = lane_of(abs(kx), top)
            lane = lane % (top // 2) + (lane // (top // 2)) * top
            pick[r, lane, j] = 1.0
            pick[r, lane + top // 2, LANES + j] = 1.0 if kx > 0 else -1.0
    turn = np.zeros((2, top, top), np.float32)
    for i in range(top):
        turn[0, i, top - 1 - i] = 1.0
        if i:
            turn[1, i, i - 1] = 1.0
    return round_bf(pick), round_bf(turn)


def send(src, dst, sems, at, device):
    copy = pltpu.make_async_remote_copy(
        src_ref=src,
        dst_ref=dst,
        send_sem=sems[0].at[at],
        recv_sem=sems[1].at[at],
        device_id=device,
        device_id_type=MESH,
    )
    copy.start()
    return copy


def greet(devices):
    barrier = pltpu.get_barrier_semaphore()
    for device in devices:
        pl.semaphore_signal(barrier, inc=1, device_id=device, device_id_type=MESH)
    return lambda: pl.semaphore_wait(barrier, len(devices))


def row_places(nrows):
    r = lax.axis_index("rows")
    core = lax.rem(r, 2)
    mate = {"rows": r + 1 - 2 * core}
    others = [{"rows": lax.rem(r + 2 * d, nrows)} for d in range(1, nrows // 2)]
    return r, core, mate, others


def expanded(flags):
    rows, tiles = flags.shape
    return jnp.concatenate(
        [jnp.broadcast_to(flags[:, j : j + 1], (rows, TILE)) for j in range(tiles)], axis=1
    )


def transposed_line(columns):
    return jnp.sum(columns.T, axis=0, keepdims=True)


def as_tail(*rows):
    shape = (TAIL, rows[0].shape[1])
    row = lax.broadcasted_iota(jnp.int32, shape, 0)
    tail = jnp.zeros(shape, F32)
    for i, v in enumerate(rows):
        tail = jnp.where(row == i, jnp.broadcast_to(v, shape), tail)
    return tail


def store_blocks(part, sums, tail=None):
    blocks = part.shape[0]
    share = sums.shape[0] // blocks
    for b in range(blocks):
        part[b, :share] = sums[b * share : (b + 1) * share].astype(BF)
        if tail is not None:
            part[b, share:] = tail.astype(BF)


def lane_sums(values):
    total = values[:, :LANES]
    for i in range(LANES, values.shape[1], LANES):
        total = total + values[:, i : i + LANES]
    return total


def kernel(
    sizes, names,
    sims_ref, data_ref, mask_ref, bins_ref, signal_ref, noise_ref, norm_ref, matching_ref,
    fy_ref, cs_ref, rows_ref, cols_ref, ty_ref, ft_ref, fx_ref, ts_ref, pick_ref, turn_ref,
    out_ref,
    *scratch,
):
    nrows, nreal, nfield, unit, step = sizes
    s = types.SimpleNamespace(**dict(zip(names, scratch)))
    h, kf = s.ty.shape
    top, quarter, half = kf // 2, kf // 4, s.even.shape[1]
    cols = bins_ref.shape[1]
    nbins = norm_ref.shape[1]
    r, core, mate, others = row_places(nrows)
    y, chips = r // 2, nrows // 2
    real = lax.axis_index("real")
    field = lax.axis_index("field")
    along_real = [{"real": lax.rem(real + d, nreal)} for d in range(1, nreal)]
    along_rows = [{"rows": lax.rem(r + d, nrows)} for d in range(1, nrows)]
    along_field = [{"field": lax.rem(field + d, nfield)} for d in range(1, nfield)]
    share = top // chips

    block_of = core * chips + y
    from_chip = [core * chips + lax.rem(y - d + chips, chips) for d in range(chips)]

    copies = {}
    tiles = h // TILE
    for m, src in enumerate((sims_ref, data_ref)):
        for t in range(tiles):
            rows = pl.ds(t * TILE, TILE)
            copies[m, t] = pltpu.make_async_copy(
                src.at[rows], s.maps.at[m, rows], s.map_sem.at[m, t]
            )
    for i, (name, src, dst) in enumerate(
        [("fy", fy_ref, s.fy), ("cs", cs_ref.at[r], s.cs), ("rows", rows_ref, s.rows),
         ("cols", cols_ref, s.cols), ("ty", ty_ref.at[r], s.ty), ("ft", ft_ref, s.ft),
         ("fx", fx_ref, s.fx), ("ts", ts_ref.at[r], s.ts), ("pick", pick_ref.at[r], s.pick),
         ("turn", turn_ref, s.turn)]
    ):
        copies[name] = pltpu.make_async_copy(src, dst, s.load_sem.at[i])

    def load(*which):
        for name in which:
            copies[name].start()

    def loaded(*which):
        for name in which:
            copies[name].wait()

    load(*((0, t) for t in range(tiles)), "fy", "cs")
    arrived = greet(along_real + along_rows + along_field)


    def bins_out():
        s.bins[r] = bins_ref[...].astype(F32).astype(BF)
        return [
            send(s.bins.at[r], s.bins.at[r], (s.sbf, s.rbf), d, device)
            for d, device in enumerate(others)
        ]

    def bins_on(copies):
        for copy in copies:
            copy.wait()
        blocks = [lax.rem(r + 2 * d, nrows) for d in range(chips)]
        return [
            send(s.bins.at[block], s.bins.at[block], (s.sbm, s.rbm), d, mate)
            for d, block in enumerate(blocks)
        ]

    def take(t, idx):
        table = jnp.broadcast_to(s.tab[t : t + 1, :], (idx.shape[0], LANES))
        parts = [
            jnp.take_along_axis(table[:, : idx.shape[1]] if idx.shape[1] < LANES else table,
                                idx[:, i : i + LANES], axis=1, mode="promise_in_bounds")
            for i in range(0, idx.shape[1], LANES)
        ]
        return parts[0] if len(parts) == 1 else jnp.concatenate(parts, axis=1)

    def filter_cells():
        weight = 1.0 / (signal_ref[...] + noise_ref[...])
        s.tab[...] = jnp.zeros_like(s.tab)
        s.tab[0:1, :nbins] = 4.0 * weight
        s.tab[1:2, :nbins] = 4.0 * (signal_ref[...] * weight)
        s.tab[2:3, :nbins] = 2.0 * norm_ref[...]
        s.ncell[...] = take(2, bins_ref[...])
        by_row = [
            jnp.dot(s.rows[...], s.bins[i], preferred_element_type=F32).astype(BF) for i in range(nrows)
        ]
        by_row = jnp.concatenate(by_row, axis=1)
        cells = jnp.dot(by_row, s.cols[...], preferred_element_type=F32)
        row = lax.broadcasted_iota(jnp.int32, cells.shape, 0)
        lane = lax.broadcasted_iota(jnp.int32, cells.shape, 1)
        absent = (row == top - 1) | (lane == quarter - 1)
        s.idx[...] = jnp.where(absent, nbins, cells.astype(jnp.int32))
        s.by_row[...] = by_row

    def filters(t):
        shape = (top, top)
        ky = lax.broadcasted_iota(jnp.int32, shape, 0) + 1
        at = lax.broadcasted_iota(jnp.int32, shape, 1)
        kx = jnp.where(at < quarter, 2 * at + 2, 2 * (at - quarter) + 1)
        ly, lx = ky.astype(F32) * step, kx.astype(F32) * step
        v = take(t, s.idx[...])
        pp, pm = v[:top, :top], v[:top, top:]
        mp, mm = v[top:kf, :top], v[top:kf, top:]
        a, b = (pp + mm) + (mp + pm), (pp + mm) - (mp + pm)
        zero_row = (v[kf : kf + 1, :top] + v[kf : kf + 1, top:]) * unit
        hot = (lax.broadcasted_iota(jnp.int32, (TAIL, kf), 1) == top).astype(F32).astype(BF)
        line = lax.dot_general(hot, s.by_row[:kf], NT, preferred_element_type=F32)
        lane = lax.broadcasted_iota(jnp.int32, (TAIL, kf), 1)
        line = take(t, jnp.where(lane == top - 1, nbins, line.astype(jnp.int32)))[:1]
        line = line[:, :top] + line[:, top:]
        if t == 0:
            s.tabs[0] = a
            s.tabs[1] = b
            dc = take(0, s.by_row[kf:, top : top + LANES].astype(F32).astype(jnp.int32))[:1]
            dc = jnp.where(lax.broadcasted_iota(jnp.int32, dc.shape, 1) == 0, dc * unit, 0.0)
            s.lines[0:1, :top] = zero_row
            s.lines[1:2, :] = jnp.concatenate([line, line], axis=1)
            s.lines[3:4, :LANES] = dc
        else:
            s.tabs[2] = lx * a
            s.tabs[3] = lx * b
            s.tabs[4] = ly * a
            s.tabs[5] = ly * b
            ly_row = (lax.broadcasted_iota(jnp.int32, (1, top), 1) + 1).astype(F32) * step
            s.lines[0:1, top:] = zero_row * lx[:1]
            s.lines[2:3, :] = jnp.concatenate([ly_row * line, -(ly_row * line)], axis=1)


    def fold(m):
        for t in range(tiles):
            loaded((m, t))
            rows = pl.ds(t * TILE, TILE)
            flags = s.mask[t]
            lo = s.maps[m, rows, :half].astype(F32) * flags[:, :half]
            hi = s.maps[m, rows, half:].astype(F32) * flags[:, half:]
            both = lo + hi
            s.even[rows, :] = both.astype(BF)
            s.odd[rows, :] = (lo - hi).astype(BF)
            s.zero_b[rows, :] = (lane_sums(both) * unit).astype(BF)

    def columns(m, q):
        side = s.odd if q else s.even
        out = jnp.dot(side[...], s.fy[q], preferred_element_type=F32)
        s.cells[...] = out.astype(BF)
        sums = jnp.dot(s.cs[...], s.cells[...], preferred_element_type=F32)
        for i in range(2):
            at = 2 * q + i
            s.edge[m, at : at + 1] = sums[kf : kf + 1, i * quarter : (i + 1) * quarter]
        if q == 0:
            line = jnp.dot(s.cs[...], s.zero_b[...], preferred_element_type=F32)
            turned = transposed_line(line[:kf])
            for i in range(4):
                s.edge[m, 4 + i : 5 + i] = turned[:, i * quarter : (i + 1) * quarter]
            s.edge[m, 8:9] = line[kf : kf + 1]
        store_blocks(s.fpart.at[m, q], sums[:kf])
        return send(
            s.fpart.at[m, q, half_of(1 - core)], s.fmate.at[m, q], (s.sf1, s.rf1), (m, q), mate
        )


    def edges_out(m):
        s.edge_out[m] = s.edge[m].astype(BF)
        return [
            send(s.edge_out.at[m], s.edge_in.at[m, d], (s.se, s.re), (m, d), device)
            for d, device in enumerate(along_rows)
        ]

    def edges_done(m, copies):
        total = s.edge[m]
        for d, copy in enumerate(copies):
            copy.wait()
            total = total + s.edge_in[m, d].astype(F32)
        s.edge[m] = total
        if m == 0:
            s.edge_z[...] = total.astype(BF)

    half_of = lambda c: pl.ds(c * chips, chips)

    def cells_to_chips(m, q, first):
        first.wait()
        s.fchip[m, q] = (s.fpart[m, q, half_of(core)].astype(F32) + s.fmate[m, q].astype(F32)).astype(BF)
        return [
            send(s.fchip.at[m, q, lax.rem(y + d + 1, chips)], s.ffar.at[m, q, d], (s.sf2, s.rf2), (m, q, d), device)
            for d, device in enumerate(others)
        ]

    def cells_done(m, q, copies):
        total = s.fchip[m, q, y].astype(F32)
        for d, copy in enumerate(copies):
            copy.wait()
            total = total + s.ffar[m, q, d].astype(F32)
        s.pq[m, q, block_of] = total.astype(BF)
        return gather_out(m, q)


    def gather_out(m, q):
        sends = lambda sems, at, device: send(
            s.pq.at[m, q, block_of], s.pq.at[m, q, block_of], sems, (m, q, at), device
        )
        far = [sends((s.sgf, s.rgf), d, device) for d, device in enumerate(others)]
        return far, [sends((s.sgm, s.rgm), 0, mate)]

    def gather_on(m, q, copies):
        far, near = copies
        for d, copy in enumerate(far):
            copy.wait()
            block = from_chip[d + 1]
            near.append(
                send(s.pq.at[m, q, block], s.pq.at[m, q, block], (s.sgm, s.rgm), (m, q, d + 1), mate)
            )
        return near

    def finish(copies):
        for copy in copies:
            copy.wait()


    def partner_out(q):
        return [
            send(s.pq.at[0, q, block_of], s.zin.at[q, d], (s.sz, s.rz), (q, d), device)
            for d, device in enumerate(along_real)
        ]

    def partner_edges_out():
        return [
            send(s.edge_z, s.edge_zin.at[d], (s.sez, s.rez), d, device)
            for d, device in enumerate(along_real)
        ]

    def partner_edges(copies):
        partner = matching_ref[real]
        named = lambda d: jnp.where(lax.rem(real - d + nreal, nreal) == partner, 1.0, 0.0)
        total = named(0) * s.edge[0]
        for d, copy in enumerate(copies):
            copy.wait()
            total = total + named(d + 1) * s.edge_zin[d].astype(F32)
        s.edge[2] = total

    def partner_on(q, copies):
        partner = matching_ref[real]
        named = lambda d: jnp.where(lax.rem(real - d + nreal, nreal) == partner, 1.0, 0.0)
        total = named(0) * s.pq[0, q, block_of].astype(F32)
        for d, copy in enumerate(copies):
            copy.wait()
            total = total + named(d + 1) * s.zin[q, d].astype(F32)
        s.pq[2, q, block_of] = total.astype(BF)
        return gather_out(2, q)

    def make_y(m, q, slot):
        at = slice(q * quarter, (q + 1) * quarter)
        for b in range(chips):
            rows = slice(b * share, (b + 1) * share)
            p_re, p_im, q_re, q_im = (
                s.pq[m, q, c * chips + b, :, i * quarter : (i + 1) * quarter].astype(F32)
                for c in range(2)
                for i in range(2)
            )
            aw, bw, xa, xb, ya, yb = (s.tabs[i, rows, at] for i in range(6))
            sets = (
                (aw * p_re + bw * q_im, aw * p_im - bw * q_re, aw * q_re - bw * p_im, aw * q_im + bw * p_re),
                (xb * q_re - xa * p_im, xb * q_im + xa * p_re, -(xb * p_re) - xa * q_im, xa * q_re - xb * p_im),
                (ya * q_re - yb * p_im, ya * q_im + yb * p_re, -(ya * p_re) - yb * q_im, yb * q_re - ya * p_im),
            )
            for leg, values in enumerate(sets):
                for i, v in enumerate(values):
                    where = (i % 2) * quarter
                    row = (i // 2) * top + b * share
                    s.zbuf[leg, row : row + share, where : where + quarter] = v.astype(BF)
        w_row = s.lines[0:1, q * quarter : (q + 1) * quarter]
        g_row = s.lines[0:1, top + q * quarter : top + (q + 1) * quarter]
        re, im = s.edge[m, 2 * q : 2 * q + 1], s.edge[m, 2 * q + 1 : 2 * q + 2]
        zero_rows = (
            jnp.concatenate([w_row * re, w_row * im], axis=1),
            jnp.concatenate([-(g_row * im), g_row * re], axis=1),
            None,
        )
        for leg in range(3):
            out = jnp.dot(s.ty[...], s.zbuf[leg], preferred_element_type=F32)
            if zero_rows[leg] is not None:
                out = out + zero_rows[leg]
            s.ybuf[slot, q, leg] = out.astype(BF)
        if q == 0:
            line = [s.edge[m, 4 + i : 5 + i] for i in range(4)]
            b_line = s.lines[1:2, :] * jnp.concatenate(line, axis=1)
            y_line = s.lines[2:3, :] * jnp.concatenate(line[2:] + line[:2], axis=1)
            row = lax.broadcasted_iota(jnp.int32, (LANES, kf), 0)
            both = jnp.where(row == 0, b_line, jnp.where(row == 1, y_line, 0.0)).astype(BF)
            col = lax.dot_general(s.ty[...], both, NT, preferred_element_type=F32)
            dc = jnp.sum(s.edge[m, 8:9], axis=1, keepdims=True) * s.lines[3:4, :LANES]
            s.ycol[slot] = (col + dc) * unit

    def legs_done(slot, q):
        dest = s.other if slot else s.own_legs
        for leg in range(3):
            for here in (slice(at, at + CHUNK) for at in range(0, half, CHUNK)):
                out = jnp.dot(s.ybuf[slot, q, leg], s.ft[q, :, here], preferred_element_type=F32)
                if q == 0 and leg != 1:
                    lane = 0 if leg == 0 else 1
                    out = out + s.ycol[slot, :, lane : lane + 1]
                dest[leg, q, :, here] = out.astype(BF)

    def products():
        rows_of = 16

        @pl.loop(0, h // rows_of)
        def _(c):
            rows = pl.ds(pl.multiple_of(c * rows_of, rows_of), rows_of)
            total = jnp.zeros((rows_of, LANES), F32)
            for here in (slice(at, at + CHUNK) for at in range(0, half, CHUNK)):
                o = [[s.own_legs[leg, q, rows, here] for q in range(2)] for leg in range(3)]
                t = [[s.other[leg, q, rows, here] for q in range(2)] for leg in range(3)]
                for i, leg in enumerate((1, 2)):
                    for q in range(2):
                        out = (t[leg][0] * o[0][q] + t[leg][1] * o[0][1 - q]) + (
                            o[leg][0] * t[0][q] + o[leg][1] * t[0][1 - q]
                        )
                        s.prods[i, q, rows, here] = out
                        if q == 0 and i == 1:
                            total = total + lane_sums(out.astype(F32))
            s.zero[rows, :] = total

    def pair_cells(e):
        q = e % 2
        for i, table in enumerate((s.fx, s.fy)):
            out = jnp.dot(s.prods[i, q], table[q], preferred_element_type=F32)
            s.wbuf[q, i * h : (i + 1) * h, :] = out.astype(BF)

    def pair_sums(e):
        q = e % 2
        sums = jnp.dot(s.ts[...], s.wbuf[q], preferred_element_type=F32)
        rows = [sums[kf : kf + 1]]
        if q == 1:
            column = (s.zero[...] * unit).astype(BF)
            line = transposed_line(jnp.dot(s.ts[:kf, h:], column, preferred_element_type=F32))
            rows += [line[:, :top], line[:, top:]]
        store_blocks(s.part.at[e], sums[:kf], as_tail(*rows))

    a_rows, b_rows = pl.ds(0, top // 2), pl.ds(top // 2, top // 2 + TAIL)

    def to_mate(e):
        return send(s.part.at[e, 1 - core], s.mate_in.at[e], (s.s1, s.r1), e, mate)

    def first_out(e, copy):
        copy.wait()
        s.chip[e] = (s.part[e, core].astype(F32) + s.mate_in[e].astype(F32)).astype(BF)
        a = [
            send(s.chip.at[e, a_rows], s.a_field.at[e, d], (s.saf, s.raf), (e, d), device)
            for d, device in enumerate(along_field)
        ]
        b = [
            send(s.chip.at[e, b_rows], s.b_far.at[e, d], (s.sby, s.rby), (e, d), device)
            for d, device in enumerate(others)
        ]
        return a, b

    def gathered(total, copies, slots):
        total = total.astype(F32)
        for d, copy in enumerate(copies):
            copy.wait()
            total = total + slots(d).astype(F32)
        return total.astype(BF)

    def second_out(e, copies):
        a, b = copies
        s.mid[e, a_rows] = gathered(s.chip[e, a_rows], a, lambda d: s.a_field[e, d])
        a = [
            send(s.mid.at[e, a_rows], s.a_far.at[e, d], (s.say, s.ray), (e, d), device)
            for d, device in enumerate(others)
        ]
        s.mid[e, b_rows] = gathered(s.chip[e, b_rows], b, lambda d: s.b_far[e, d])
        b = [
            send(s.mid.at[e, b_rows], s.b_field.at[e, d], (s.sbfield, s.rbfield), (e, d), device)
            for d, device in enumerate(along_field)
        ]
        return a, b

    def last_out(e, copies):
        a, b = copies
        s.fin[e, core, a_rows] = gathered(s.mid[e, a_rows], a, lambda d: s.a_far[e, d])
        s.fin[e, core, b_rows] = gathered(s.mid[e, b_rows], b, lambda d: s.b_field[e, d])
        return send(s.fin.at[e, core], s.fin.at[e, core], (s.s3, s.r3), e, mate)

    def each(step, pair, state=None):
        return [
            step(2 * pair + q) if state is None else step(2 * pair + q, state[q]) for q in range(2)
        ]

    def assemble(pair, copies):
        picked = [0.0, 0.0, 0.0]
        for q in range(2):
            e = 2 * pair + q
            copies[q].wait()
            tail = s.fin[e, 0, top:]
            if q == 1:
                lines = [tail.astype(F32)[1:2], tail.astype(F32)[2:3]]
            for i, v in enumerate((s.fin[e, 0, :top], s.fin[e, 1, :top], tail)):
                chosen = s.pick[q * top : (q + 1) * top, :]
                picked[i] = picked[i] + jnp.dot(v, chosen, preferred_element_type=F32)
        zero_line = picked[2][:1]
        column = jnp.broadcast_to(jnp.concatenate(lines, axis=1), (LANES, kf)).T
        lane = lax.broadcasted_iota(jnp.int32, (kf, LANES), 1)
        column = jnp.where(lane + r * cols == top, column, 0.0)
        p_re, p_im = picked[0][:, :LANES] + column[:top], picked[0][:, LANES:]
        q_re, q_im = picked[1][:, :LANES] + column[top:], picked[1][:, LANES:]
        plus = jnp.concatenate([p_re + q_im, p_im - q_re], axis=1).astype(BF)
        minus = jnp.concatenate([p_re - q_im, p_im + q_re], axis=1).astype(BF)
        lower = jnp.dot(s.turn[0], minus, preferred_element_type=F32)
        upper = jnp.dot(s.turn[1], plus, preferred_element_type=F32)
        row = lax.broadcasted_iota(jnp.int32, upper.shape, 0)
        upper = jnp.where(row == 0, zero_line, upper)
        for i in range(2):
            at = slice(i * LANES, i * LANES + cols)
            s.out[pair, i, :top] = (lower[:, at] * s.ncell[:top]).astype(BF)
            s.out[pair, i, top:] = (upper[:, at] * s.ncell[top:]).astype(BF)
        copy = pltpu.make_async_copy(s.out.at[pair], out_ref.at[pair], s.out_sem.at[pair])
        copy.start()
        return copy

    full = expanded(mask_ref[...].astype(F32))
    for t in range(full.shape[0]):
        s.mask[t] = full[t : t + 1]
    s.edge[...] = jnp.zeros_like(s.edge)
    fold(0)
    arrived()
    bins = bins_out()
    load(*((1, t) for t in range(tiles)), "rows", "cols")
    loaded("fy", "cs")
    own, data = [columns(0, 0)], []
    own.append(columns(0, 1))
    own_edges = edges_out(0)
    fold(1)
    load("ty", "ft", "fx", "ts", "pick", "turn")
    own[0] = cells_to_chips(0, 0, own[0])
    data.append(columns(1, 0))
    own[1] = cells_to_chips(0, 1, own[1])
    bins = bins_on(bins)
    data.append(columns(1, 1))
    data_edges = edges_out(1)
    loaded("rows", "cols")
    own[0] = cells_done(0, 0, own[0])
    finish(bins)
    filter_cells()
    edges_done(0, own_edges)
    edges = partner_edges_out()
    own[1] = cells_done(0, 1, own[1])
    partner = [partner_out(0)]
    data[0] = cells_to_chips(1, 0, data[0])
    filters(0)
    partner.append(partner_out(1))
    data[1] = cells_to_chips(1, 1, data[1])
    filters(1)
    edges_done(1, data_edges)
    own[0] = gather_on(0, 0, own[0])
    loaded("ty", "ft")
    finish(own[0])
    make_y(0, 0, 0)
    own[1] = gather_on(0, 1, own[1])
    data[0] = cells_done(1, 0, data[0])
    legs_done(0, 0)
    data[1] = cells_done(1, 1, data[1])
    finish(own[1])
    make_y(0, 1, 0)
    data[0] = gather_on(1, 0, data[0])
    legs_done(0, 1)
    data[1] = gather_on(1, 1, data[1])
    finish(data[0])
    make_y(1, 0, 1)
    legs_done(1, 0)
    partner[0] = partner_on(0, partner[0])
    partner_edges(edges)
    finish(data[1])
    make_y(1, 1, 1)
    legs_done(1, 1)
    partner[1] = partner_on(1, partner[1])
    products()
    partner[0] = gather_on(2, 0, partner[0])
    loaded("fx", "ts", "pick", "turn")
    pair_cells(0)
    pair_sums(0)
    ds = [to_mate(0)]
    partner[1] = gather_on(2, 1, partner[1])
    pair_cells(1)
    ds[0] = first_out(0, ds[0])
    pair_sums(1)
    ds.append(to_mate(1))
    finish(partner[0])
    make_y(2, 0, 1)
    legs_done(1, 0)
    ds[1] = first_out(1, ds[1])
    finish(partner[1])
    make_y(2, 1, 1)
    ds[0] = second_out(0, ds[0])
    legs_done(1, 1)
    products()
    ds[1] = second_out(1, ds[1])
    pair_cells(2)
    pair_sums(2)
    ss = [to_mate(2)]
    pair_cells(3)
    ss[0] = first_out(2, ss[0])
    pair_sums(3)
    ss.append(to_mate(3))
    ds = each(last_out, 0, ds)
    ss[1] = first_out(3, ss[1])
    ss[0] = second_out(2, ss[0])
    ds = assemble(0, ds)
    ss[1] = second_out(3, ss[1])
    ss = each(last_out, 1, ss)
    assemble(1, ss).wait()
    ds.wait()


def estimates(sims, data, mask_flags, bins, signal, noise, norm, matching, nrows, nreal, nfield):
    h, npix = sims.shape
    kf, cols = bins.shape
    top, half = kf // 2, npix // 2
    t = constants(npix, kf, nrows)
    rows, pick_cols = cell_tables(kf)
    pick, turn = output_tables(kf, nrows)
    far, fields = max(nrows // 2 - 1, 1), max(nfield - 1, 1)
    chips = nrows // 2
    share = top // chips
    piece, block = (share, top), (top + TAIL, top)
    a_block, b_block = (top // 2, top), (top // 2 + TAIL, top)
    buf = lambda *shape: pltpu.VMEM(shape, BF)
    wide = lambda *shape: pltpu.VMEM(shape, F32)
    dma = lambda *shape: pltpu.SemaphoreType.DMA(shape)
    scratch = dict(
        maps=buf(2, h, npix), fy=buf(2, half, top), cs=buf(kf + TAIL, h), rows=buf(kf + TAIL, kf),
        cols=buf(kf, kf), ty=buf(h, kf), ft=buf(2, top, half), fx=buf(2, half, top),
        ts=buf(kf + TAIL, 2 * h), pick=buf(kf, 2 * LANES), turn=buf(2, top, top),
        idx=pltpu.VMEM((kf + TAIL, kf), jnp.int32), by_row=buf(kf + TAIL, kf),
        mask=wide(h // TILE, 1, npix), bins=buf(nrows, kf, cols), tab=wide(8, LANES),
        tabs=wide(6, top, top), lines=wide(8, kf),
        even=buf(h, half), odd=buf(h, half), zero_b=buf(h, LANES), cells=buf(h, top),
        fpart=buf(2, 2, nrows, *piece), fmate=buf(2, 2, chips, *piece), fchip=buf(2, 2, chips, *piece),
        ffar=buf(2, 2, far, *piece), pq=buf(3, 2, nrows, *piece), zin=buf(2, nreal - 1, *piece),
        ybuf=buf(2, 2, 3, h, top), ycol=wide(2, h, LANES), zbuf=buf(3, kf, top),
        own_legs=buf(3, 2, h, half), other=buf(3, 2, h, half), prods=buf(2, 2, h, half),
        zero=wide(h, LANES), wbuf=buf(2, 2 * h, top), ncell=wide(kf, cols),
        part=buf(4, 2, *block), mate_in=buf(4, *block), chip=buf(4, *block),
        a_field=buf(4, fields, *a_block), b_far=buf(4, far, *b_block), mid=buf(4, *block),
        a_far=buf(4, far, *a_block), b_field=buf(4, fields, *b_block), fin=buf(4, 2, *block),
        out=buf(2, 2, kf, cols), out_sem=dma(2), load_sem=dma(10), map_sem=dma(2, h // TILE), sbf=dma(far), rbf=dma(far), sbm=dma(chips), rbm=dma(chips),
        sf1=dma(2, 2), rf1=dma(2, 2), sf2=dma(2, 2, far), rf2=dma(2, 2, far),
        sgf=dma(3, 2, far), rgf=dma(3, 2, far), sgm=dma(3, 2, chips), rgm=dma(3, 2, chips),
        edge=wide(3, TAIL, LANES), edge_out=buf(2, TAIL, LANES), edge_in=buf(2, nrows - 1, TAIL, LANES),
        edge_z=buf(TAIL, LANES), edge_zin=buf(nreal - 1, TAIL, LANES),
        se=dma(2, nrows - 1), re=dma(2, nrows - 1), sez=dma(nreal - 1), rez=dma(nreal - 1),
        sz=dma(2, nreal - 1), rz=dma(2, nreal - 1),
        s1=dma(4), r1=dma(4), saf=dma(4, fields), raf=dma(4, fields),
        sbfield=dma(4, fields), rbfield=dma(4, fields),
        say=dma(4, far), ray=dma(4, far), sby=dma(4, far), rby=dma(4, far), s3=dma(4), r3=dma(4),
    )
    hbm = pl.BlockSpec(memory_space=pl.ANY)
    vmem = pl.BlockSpec(memory_space=pltpu.VMEM)
    smem = pl.BlockSpec(memory_space=pltpu.SMEM)
    tables = [t["fy"], t["cs"], rows, pick_cols, t["ty"], t["ft"], t["fx"], t["ts"], pick, turn]
    return pl.pallas_call(
        functools.partial(kernel, (nrows, nreal, nfield, t["unit"], t["step"]), tuple(scratch)),
        out_shape=jax.ShapeDtypeStruct((2, 2, kf, cols), BF),
        in_specs=[hbm] * 2 + [vmem] * 5 + [smem] + [hbm] * len(tables),
        out_specs=hbm,
        scratch_shapes=list(scratch.values()),
        compiler_params=pltpu.CompilerParams(
            collective_id=0, has_side_effects=True, vmem_limit_bytes=VMEM_LIMIT
        ),
        cost_estimate=pl.CostEstimate(
            flops=32 * h * npix * kf, bytes_accessed=24 * 2**20, transcendentals=0
        ),
    )(sims, data, mask_flags, bins, signal, noise, norm, matching, *(jnp.asarray(v) for v in tables))


def body(nrows, nreal, nfield, sims, data, mask_flags, bins, cl_signal, cl_noise, norm, matching):
    out = estimates(
        sims[0, 0], data[0], mask_flags, bins, cl_signal, cl_noise, norm[None], matching,
        nrows, nreal, nfield,
    )
    return out.astype(F32)[None]


def solution(mesh):
    in_specs = (
        P("real", "field", "rows", None),
        P("field", "rows", None),
        P("rows", None),
        P(None, "rows"),
        P("field", None),
        P("field", None),
        P(),
        P(),
    )
    out_specs = P("real", None, None, None, "rows")
    f = functools.partial(body, mesh.shape["rows"], mesh.shape["real"], mesh.shape["field"])
    return jax.shard_map(f, mesh=mesh, in_specs=in_specs, out_specs=out_specs, check_vma=False)
```

```python
import functools
import math
import types

import jax
import jax.numpy as jnp
import numpy as np
from jax import lax
from jax.experimental import pallas as pl
from jax.experimental.pallas import tpu as pltpu
from jax.sharding import PartitionSpec as P

TILE = 128
LANES = 128
TAIL = 16
CHUNK = 256
BF = jnp.bfloat16
F32 = jnp.float32
VMEM_LIMIT = 60 * 1024 * 1024
MESH = pl.DeviceIdType.MESH
NT = (((1,), (1,)), ((), ()))


def round_bf(values):
    return np.asarray(values, np.float32).astype(BF)


@functools.lru_cache
def constants(npix, kf, nrows):
    top, half, h = kf // 2, npix // 2, npix // nrows
    scale, step = npix ** -0.5, 2.0 * math.pi / npix

    def cis(pixels, freqs):
        angle = np.mod(pixels[:, None] * freqs[None, :], npix) * step
        rounded = [round_bf(f(angle) * scale).astype(np.float32) for f in (np.cos, np.sin)]
        return rounded

    x, y = np.arange(half), np.arange(npix)
    fy, fx = [], []
    for kx in (np.arange(2, top + 1, 2), np.arange(1, top, 2)):
        c, s = cis(x, kx)
        lx = kx * step
        fy.append(np.concatenate([c, -s], axis=1))
        fx.append(np.concatenate([lx * s, lx * c], axis=1))
    fy, fx = np.stack(fy), np.stack(fx)
    ky = np.arange(1, top + 1)
    c, s = (v.T for v in cis(y, ky))
    ly = (ky * step)[:, None]
    zero = np.full((1, npix), round_bf(scale).astype(np.float32))
    pad = np.zeros((TAIL - 1, npix), np.float32)
    split = lambda a: a.reshape(a.shape[0], nrows, h).transpose(1, 0, 2)
    cs = split(np.concatenate([c, s, zero, pad]))
    sy = split(np.concatenate([ly * s, -ly * c, 0 * zero, pad]))
    return dict(
        fy=round_bf(fy),
        fx=round_bf(fx),
        ft=round_bf(fy.transpose(0, 2, 1)),
        cs=round_bf(cs),
        ty=round_bf(cs[:, : 2 * top].transpose(0, 2, 1)),
        ts=round_bf(np.concatenate([cs, sy], axis=2)),
        unit=float(round_bf(scale)),
        step=step,
    )


def lane_of(k, top):
    return k // 2 - 1 if k % 2 == 0 else top // 2 + (k - 1) // 2


@functools.lru_cache
def cell_tables(kf):
    top = kf // 2
    rows = np.zeros((kf + TAIL, kf), np.float32)
    cols = np.zeros((kf, kf), np.float32)
    for k in range(1, top + 1):
        if k < top:
            rows[k - 1, top + k] = 1.0
            cols[top + k, lane_of(k, top)] = 1.0
        rows[top + k - 1, top - k] = 1.0
        cols[top - k, top + lane_of(k, top)] = 1.0
    rows[kf, top] = 1.0
    return round_bf(rows), round_bf(cols)


@functools.lru_cache
def output_tables(kf, nrows):
    top, cols = kf // 2, kf // nrows
    pick = np.zeros((nrows, kf, 2 * LANES), np.float32)
    for r in range(nrows):
        for j in range(cols):
            kx = r * cols + j - top
            if kx == 0:
                continue
            lane = lane_of(abs(kx), top)
            lane = lane % (top // 2) + (lane // (top // 2)) * top
            pick[r, lane, j] = 1.0
            pick[r, lane + top // 2, LANES + j] = 1.0 if kx > 0 else -1.0
    turn = np.zeros((2, top, top), np.float32)
    for i in range(top):
        turn[0, i, top - 1 - i] = 1.0
        if i:
            turn[1, i, i - 1] = 1.0
    return round_bf(pick), round_bf(turn)


def send(src, dst, sems, at, device):
    copy = pltpu.make_async_remote_copy(
        src_ref=src,
        dst_ref=dst,
        send_sem=sems[0].at[at],
        recv_sem=sems[1].at[at],
        device_id=device,
        device_id_type=MESH,
    )
    copy.start()
    return copy


def greet(devices):
    barrier = pltpu.get_barrier_semaphore()
    for device in devices:
        pl.semaphore_signal(barrier, inc=1, device_id=device, device_id_type=MESH)
    return lambda: pl.semaphore_wait(barrier, len(devices))


def row_places(nrows):
    r = lax.axis_index("rows")
    core = lax.rem(r, 2)
    mate = {"rows": r + 1 - 2 * core}
    others = [{"rows": lax.rem(r + 2 * d, nrows)} for d in range(1, nrows // 2)]
    return r, core, mate, others


def expanded(flags):
    rows, tiles = flags.shape
    return jnp.concatenate(
        [jnp.broadcast_to(flags[:, j : j + 1], (rows, TILE)) for j in range(tiles)], axis=1
    )


def transposed_line(columns):
    return jnp.sum(columns.T, axis=0, keepdims=True)


def as_tail(*rows):
    shape = (TAIL, rows[0].shape[1])
    row = lax.broadcasted_iota(jnp.int32, shape, 0)
    tail = jnp.zeros(shape, F32)
    for i, v in enumerate(rows):
        tail = jnp.where(row == i, jnp.broadcast_to(v, shape), tail)
    return tail


def store_blocks(part, sums, tail=None):
    blocks = part.shape[0]
    share = sums.shape[0] // blocks
    for b in range(blocks):
        part[b, :share] = sums[b * share : (b + 1) * share].astype(BF)
        if tail is not None:
            part[b, share:] = tail.astype(BF)


def lane_sums(values):
    total = values[:, :LANES]
    for i in range(LANES, values.shape[1], LANES):
        total = total + values[:, i : i + LANES]
    return total


def kernel(
    sizes, names,
    sims_ref, data_ref, mask_ref, bins_ref, signal_ref, noise_ref, norm_ref, matching_ref,
    fy_ref, cs_ref, rows_ref, cols_ref, ty_ref, ft_ref, fx_ref, ts_ref, pick_ref, turn_ref,
    out_ref,
    *scratch,
):
    nrows, nreal, nfield, unit, step = sizes
    s = types.SimpleNamespace(**dict(zip(names, scratch)))
    h, kf = s.ty.shape
    top, quarter, half = kf // 2, kf // 4, s.even.shape[1]
    cols = bins_ref.shape[1]
    nbins = norm_ref.shape[1]
    r, core, mate, others = row_places(nrows)
    y, chips = r // 2, nrows // 2
    real = lax.axis_index("real")
    field = lax.axis_index("field")
    along_real = [{"real": lax.rem(real + d, nreal)} for d in range(1, nreal)]
    along_rows = [{"rows": lax.rem(r + d, nrows)} for d in range(1, nrows)]
    along_field = [{"field": lax.rem(field + d, nfield)} for d in range(1, nfield)]
    share = top // chips

    block_of = core * chips + y
    from_chip = [core * chips + lax.rem(y - d + chips, chips) for d in range(chips)]

    copies = {}
    tiles = h // TILE
    for m, src in enumerate((sims_ref, data_ref)):
        for t in range(tiles):
            rows = pl.ds(t * TILE, TILE)
            copies[m, t] = pltpu.make_async_copy(
                src.at[rows], s.maps.at[m, rows], s.map_sem.at[m, t]
            )
    for i, (name, src, dst) in enumerate(
        [("fy0", fy_ref.at[0], s.fy.at[0]), ("fy1", fy_ref.at[1], s.fy.at[1]), ("cs", cs_ref.at[r], s.cs), ("rows", rows_ref, s.rows),
         ("cols", cols_ref, s.cols), ("ty", ty_ref.at[r], s.ty), ("ft", ft_ref, s.ft),
         ("fx", fx_ref, s.fx), ("ts", ts_ref.at[r], s.ts), ("pick", pick_ref.at[r], s.pick),
         ("turn", turn_ref, s.turn)]
    ):
        copies[name] = pltpu.make_async_copy(src, dst, s.load_sem.at[i])

    def load(*which):
        for name in which:
            copies[name].start()

    def loaded(*which):
        for name in which:
            copies[name].wait()

    load(*((0, t) for t in range(tiles)))
    arrived = greet(along_real + along_rows + along_field)


    def bins_out():
        s.bins[r] = bins_ref[...].astype(F32).astype(BF)
        return [
            send(s.bins.at[r], s.bins.at[r], (s.sbf, s.rbf), d, device)
            for d, device in enumerate(others)
        ]

    def bins_on(copies):
        for copy in copies:
            copy.wait()
        blocks = [lax.rem(r + 2 * d, nrows) for d in range(chips)]
        return [
            send(s.bins.at[block], s.bins.at[block], (s.sbm, s.rbm), d, mate)
            for d, block in enumerate(blocks)
        ]

    def take(t, idx):
        table = jnp.broadcast_to(s.tab[t : t + 1, :], (idx.shape[0], LANES))
        parts = [
            jnp.take_along_axis(table[:, : idx.shape[1]] if idx.shape[1] < LANES else table,
                                idx[:, i : i + LANES], axis=1, mode="promise_in_bounds")
            for i in range(0, idx.shape[1], LANES)
        ]
        return parts[0] if len(parts) == 1 else jnp.concatenate(parts, axis=1)

    def filter_cells():
        weight = 1.0 / (signal_ref[...] + noise_ref[...])
        s.tab[...] = jnp.zeros_like(s.tab)
        s.tab[0:1, :nbins] = 4.0 * weight
        s.tab[1:2, :nbins] = 4.0 * (signal_ref[...] * weight)
        s.tab[2:3, :nbins] = 2.0 * norm_ref[...]
        s.ncell[...] = take(2, bins_ref[...])
        by_row = [
            jnp.dot(s.rows[...], s.bins[i], preferred_element_type=F32).astype(BF) for i in range(nrows)
        ]
        by_row = jnp.concatenate(by_row, axis=1)
        cells = jnp.dot(by_row, s.cols[...], preferred_element_type=F32)
        row = lax.broadcasted_iota(jnp.int32, cells.shape, 0)
        lane = lax.broadcasted_iota(jnp.int32, cells.shape, 1)
        absent = (row == top - 1) | (lane == quarter - 1)
        s.idx[...] = jnp.where(absent, nbins, cells.astype(jnp.int32))
        s.by_row[...] = by_row

    def filters(t):
        shape = (top, top)
        ky = lax.broadcasted_iota(jnp.int32, shape, 0) + 1
        at = lax.broadcasted_iota(jnp.int32, shape, 1)
        kx = jnp.where(at < quarter, 2 * at + 2, 2 * (at - quarter) + 1)
        ly, lx = ky.astype(F32) * step, kx.astype(F32) * step
        v = take(t, s.idx[...])
        pp, pm = v[:top, :top], v[:top, top:]
        mp, mm = v[top:kf, :top], v[top:kf, top:]
        a, b = (pp + mm) + (mp + pm), (pp + mm) - (mp + pm)
        zero_row = (v[kf : kf + 1, :top] + v[kf : kf + 1, top:]) * unit
        hot = (lax.broadcasted_iota(jnp.int32, (TAIL, kf), 1) == top).astype(F32).astype(BF)
        line = lax.dot_general(hot, s.by_row[:kf], NT, preferred_element_type=F32)
        lane = lax.broadcasted_iota(jnp.int32, (TAIL, kf), 1)
        line = take(t, jnp.where(lane == top - 1, nbins, line.astype(jnp.int32)))[:1]
        line = line[:, :top] + line[:, top:]
        if t == 0:
            s.tabs[0] = a
            s.tabs[1] = b
            dc = take(0, s.by_row[kf:, top : top + LANES].astype(F32).astype(jnp.int32))[:1]
            dc = jnp.where(lax.broadcasted_iota(jnp.int32, dc.shape, 1) == 0, dc * unit, 0.0)
            s.lines[0:1, :top] = zero_row
            s.lines[1:2, :] = jnp.concatenate([line, line], axis=1)
            s.lines[3:4, :LANES] = dc
        else:
            s.tabs[2] = lx * a
            s.tabs[3] = lx * b
            s.tabs[4] = ly * a
            s.tabs[5] = ly * b
            ly_row = (lax.broadcasted_iota(jnp.int32, (1, top), 1) + 1).astype(F32) * step
            s.lines[0:1, top:] = zero_row * lx[:1]
            s.lines[2:3, :] = jnp.concatenate([ly_row * line, -(ly_row * line)], axis=1)


    def fold(m):
        for t in range(tiles):
            loaded((m, t))
            if (m, t) == (0, 0):
                load("fy0", "cs", "fy1")
            rows = pl.ds(t * TILE, TILE)
            flags = s.mask[t]
            lo = s.maps[m, rows, :half].astype(F32) * flags[:, :half]
            hi = s.maps[m, rows, half:].astype(F32) * flags[:, half:]
            both = lo + hi
            s.even[rows, :] = both.astype(BF)
            s.odd[rows, :] = (lo - hi).astype(BF)
            s.zero_b[rows, :] = (lane_sums(both) * unit).astype(BF)

    def columns(m, q):
        side = s.odd if q else s.even
        out = jnp.dot(side[...], s.fy[q], preferred_element_type=F32)
        s.cells[...] = out.astype(BF)
        sums = jnp.dot(s.cs[...], s.cells[...], preferred_element_type=F32)
        for i in range(2):
            at = 2 * q + i
            s.edge[m, at : at + 1] = sums[kf : kf + 1, i * quarter : (i + 1) * quarter]
        store_blocks(s.fpart.at[m, q], sums[:kf])
        return send(
            s.fpart.at[m, q, half_of(1 - core)], s.fmate.at[m, q], (s.sf1, s.rf1), (m, q), mate
        )


    def edges_out(m):
        line = jnp.dot(s.cs[...], s.zero_b[...], preferred_element_type=F32)
        turned = transposed_line(line[:kf])
        for i in range(4):
            s.edge[m, 4 + i : 5 + i] = turned[:, i * quarter : (i + 1) * quarter]
        s.edge[m, 8:9] = line[kf : kf + 1]
        s.edge_out[m] = s.edge[m].astype(BF)
        return [
            send(s.edge_out.at[m], s.edge_in.at[m, d], (s.se, s.re), (m, d), device)
            for d, device in enumerate(along_rows)
        ]

    def edges_done(m, copies):
        total = s.edge[m]
        for d, copy in enumerate(copies):
            copy.wait()
            total = total + s.edge_in[m, d].astype(F32)
        s.edge[m] = total
        if m == 0:
            s.edge_z[...] = total.astype(BF)

    half_of = lambda c: pl.ds(c * chips, chips)

    def cells_to_chips(m, q, first):
        first.wait()
        s.fchip[m, q] = (s.fpart[m, q, half_of(core)].astype(F32) + s.fmate[m, q].astype(F32)).astype(BF)
        return [
            send(s.fchip.at[m, q, lax.rem(y + d + 1, chips)], s.ffar.at[m, q, d], (s.sf2, s.rf2), (m, q, d), device)
            for d, device in enumerate(others)
        ]

    def cells_done(m, q, copies):
        total = s.fchip[m, q, y].astype(F32)
        for d, copy in enumerate(copies):
            copy.wait()
            total = total + s.ffar[m, q, d].astype(F32)
        s.pq[m, q, block_of] = total.astype(BF)
        return gather_out(m, q)


    def gather_out(m, q):
        sends = lambda sems, at, device: send(
            s.pq.at[m, q, block_of], s.pq.at[m, q, block_of], sems, (m, q, at), device
        )
        far = [sends((s.sgf, s.rgf), d, device) for d, device in enumerate(others)]
        return far, [sends((s.sgm, s.rgm), 0, mate)]

    def gather_on(m, q, copies):
        far, near = copies
        for d, copy in enumerate(far):
            copy.wait()
            block = from_chip[d + 1]
            near.append(
                send(s.pq.at[m, q, block], s.pq.at[m, q, block], (s.sgm, s.rgm), (m, q, d + 1), mate)
            )
        return near

    def finish(copies):
        for copy in copies:
            copy.wait()


    def partner_out(q):
        return [
            send(s.pq.at[0, q, block_of], s.zin.at[q, d], (s.sz, s.rz), (q, d), device)
            for d, device in enumerate(along_real)
        ]

    def partner_edges_out():
        return [
            send(s.edge_z, s.edge_zin.at[d], (s.sez, s.rez), d, device)
            for d, device in enumerate(along_real)
        ]

    def partner_edges(copies):
        partner = matching_ref[real]
        named = lambda d: jnp.where(lax.rem(real - d + nreal, nreal) == partner, 1.0, 0.0)
        total = named(0) * s.edge[0]
        for d, copy in enumerate(copies):
            copy.wait()
            total = total + named(d + 1) * s.edge_zin[d].astype(F32)
        s.edge[2] = total

    def partner_on(q, copies):
        partner = matching_ref[real]
        named = lambda d: jnp.where(lax.rem(real - d + nreal, nreal) == partner, 1.0, 0.0)
        total = named(0) * s.pq[0, q, block_of].astype(F32)
        for d, copy in enumerate(copies):
            copy.wait()
            total = total + named(d + 1) * s.zin[q, d].astype(F32)
        s.pq[2, q, block_of] = total.astype(BF)
        return gather_out(2, q)

    def make_y(m, q, slot):
        at = slice(q * quarter, (q + 1) * quarter)
        for b in range(chips):
            rows = slice(b * share, (b + 1) * share)
            p_re, p_im, q_re, q_im = (
                s.pq[m, q, c * chips + b, :, i * quarter : (i + 1) * quarter].astype(F32)
                for c in range(2)
                for i in range(2)
            )
            aw, bw, xa, xb, ya, yb = (s.tabs[i, rows, at] for i in range(6))
            sets = (
                (aw * p_re + bw * q_im, aw * p_im - bw * q_re, aw * q_re - bw * p_im, aw * q_im + bw * p_re),
                (xb * q_re - xa * p_im, xb * q_im + xa * p_re, -(xb * p_re) - xa * q_im, xa * q_re - xb * p_im),
                (ya * q_re - yb * p_im, ya * q_im + yb * p_re, -(ya * p_re) - yb * q_im, yb * q_re - ya * p_im),
            )
            for leg, values in enumerate(sets):
                for i, v in enumerate(values):
                    where = (i % 2) * quarter
                    row = (i // 2) * top + b * share
                    s.zbuf[leg, row : row + share, where : where + quarter] = v.astype(BF)
        w_row = s.lines[0:1, q * quarter : (q + 1) * quarter]
        g_row = s.lines[0:1, top + q * quarter : top + (q + 1) * quarter]
        re, im = s.edge[m, 2 * q : 2 * q + 1], s.edge[m, 2 * q + 1 : 2 * q + 2]
        zero_rows = (
            jnp.concatenate([w_row * re, w_row * im], axis=1),
            jnp.concatenate([-(g_row * im), g_row * re], axis=1),
            None,
        )
        for leg in range(3):
            out = jnp.dot(s.ty[...], s.zbuf[leg], preferred_element_type=F32)
            if zero_rows[leg] is not None:
                out = out + zero_rows[leg]
            s.ybuf[slot, q, leg] = out.astype(BF)
        if q == 0:
            line = [s.edge[m, 4 + i : 5 + i] for i in range(4)]
            b_line = s.lines[1:2, :] * jnp.concatenate(line, axis=1)
            y_line = s.lines[2:3, :] * jnp.concatenate(line[2:] + line[:2], axis=1)
            row = lax.broadcasted_iota(jnp.int32, (LANES, kf), 0)
            both = jnp.where(row == 0, b_line, jnp.where(row == 1, y_line, 0.0)).astype(BF)
            col = lax.dot_general(s.ty[...], both, NT, preferred_element_type=F32)
            dc = jnp.sum(s.edge[m, 8:9], axis=1, keepdims=True) * s.lines[3:4, :LANES]
            s.ycol[slot] = (col + dc) * unit

    def legs_done(slot, q):
        dest = s.other if slot else s.own_legs
        for leg in range(3):
            for here in (slice(at, at + CHUNK) for at in range(0, half, CHUNK)):
                out = jnp.dot(s.ybuf[slot, q, leg], s.ft[q, :, here], preferred_element_type=F32)
                if q == 0 and leg != 1:
                    lane = 0 if leg == 0 else 1
                    out = out + s.ycol[slot, :, lane : lane + 1]
                dest[leg, q, :, here] = out.astype(BF)

    def products():
        rows_of = 16

        @pl.loop(0, h // rows_of)
        def _(c):
            rows = pl.ds(pl.multiple_of(c * rows_of, rows_of), rows_of)
            total = jnp.zeros((rows_of, LANES), F32)
            for here in (slice(at, at + CHUNK) for at in range(0, half, CHUNK)):
                o = [[s.own_legs[leg, q, rows, here] for q in range(2)] for leg in range(3)]
                t = [[s.other[leg, q, rows, here] for q in range(2)] for leg in range(3)]
                for i, leg in enumerate((1, 2)):
                    for q in range(2):
                        out = (t[leg][0] * o[0][q] + t[leg][1] * o[0][1 - q]) + (
                            o[leg][0] * t[0][q] + o[leg][1] * t[0][1 - q]
                        )
                        s.prods[i, q, rows, here] = out
                        if q == 0 and i == 1:
                            total = total + lane_sums(out.astype(F32))
            s.zero[rows, :] = total

    def pair_cells(e):
        q = e % 2
        for i, table in enumerate((s.fx, s.fy)):
            out = jnp.dot(s.prods[i, q], table[q], preferred_element_type=F32)
            s.wbuf[q, i * h : (i + 1) * h, :] = out.astype(BF)

    def pair_sums(e):
        q = e % 2
        sums = jnp.dot(s.ts[...], s.wbuf[q], preferred_element_type=F32)
        rows = [sums[kf : kf + 1]]
        if q == 1:
            column = (s.zero[...] * unit).astype(BF)
            line = transposed_line(jnp.dot(s.ts[:kf, h:], column, preferred_element_type=F32))
            rows += [line[:, :top], line[:, top:]]
        store_blocks(s.part.at[e], sums[:kf], as_tail(*rows))

    a_rows, b_rows = pl.ds(0, top // 2), pl.ds(top // 2, top // 2 + TAIL)

    def to_mate(e):
        return send(s.part.at[e, 1 - core], s.mate_in.at[e], (s.s1, s.r1), e, mate)

    def first_out(e, copy):
        copy.wait()
        s.chip[e] = (s.part[e, core].astype(F32) + s.mate_in[e].astype(F32)).astype(BF)
        a = [
            send(s.chip.at[e, a_rows], s.a_field.at[e, d], (s.saf, s.raf), (e, d), device)
            for d, device in enumerate(along_field)
        ]
        b = [
            send(s.chip.at[e, b_rows], s.b_far.at[e, d], (s.sby, s.rby), (e, d), device)
            for d, device in enumerate(others)
        ]
        return a, b

    def gathered(total, copies, slots):
        total = total.astype(F32)
        for d, copy in enumerate(copies):
            copy.wait()
            total = total + slots(d).astype(F32)
        return total.astype(BF)

    def second_out(e, copies):
        a, b = copies
        s.mid[e, a_rows] = gathered(s.chip[e, a_rows], a, lambda d: s.a_field[e, d])
        a = [
            send(s.mid.at[e, a_rows], s.a_far.at[e, d], (s.say, s.ray), (e, d), device)
            for d, device in enumerate(others)
        ]
        s.mid[e, b_rows] = gathered(s.chip[e, b_rows], b, lambda d: s.b_far[e, d])
        b = [
            send(s.mid.at[e, b_rows], s.b_field.at[e, d], (s.sbfield, s.rbfield), (e, d), device)
            for d, device in enumerate(along_field)
        ]
        return a, b

    def last_out(e, copies):
        a, b = copies
        s.fin[e, core, a_rows] = gathered(s.mid[e, a_rows], a, lambda d: s.a_far[e, d])
        s.fin[e, core, b_rows] = gathered(s.mid[e, b_rows], b, lambda d: s.b_field[e, d])
        return send(s.fin.at[e, core], s.fin.at[e, core], (s.s3, s.r3), e, mate)

    def each(step, pair, state=None):
        return [
            step(2 * pair + q) if state is None else step(2 * pair + q, state[q]) for q in range(2)
        ]

    def assemble(pair, copies):
        picked = [0.0, 0.0, 0.0]
        for q in range(2):
            e = 2 * pair + q
            copies[q].wait()
            tail = s.fin[e, 0, top:]
            if q == 1:
                lines = [tail.astype(F32)[1:2], tail.astype(F32)[2:3]]
            for i, v in enumerate((s.fin[e, 0, :top], s.fin[e, 1, :top], tail)):
                chosen = s.pick[q * top : (q + 1) * top, :]
                picked[i] = picked[i] + jnp.dot(v, chosen, preferred_element_type=F32)
        zero_line = picked[2][:1]
        column = jnp.broadcast_to(jnp.concatenate(lines, axis=1), (LANES, kf)).T
        lane = lax.broadcasted_iota(jnp.int32, (kf, LANES), 1)
        column = jnp.where(lane + r * cols == top, column, 0.0)
        p_re, p_im = picked[0][:, :LANES] + column[:top], picked[0][:, LANES:]
        q_re, q_im = picked[1][:, :LANES] + column[top:], picked[1][:, LANES:]
        plus = jnp.concatenate([p_re + q_im, p_im - q_re], axis=1).astype(BF)
        minus = jnp.concatenate([p_re - q_im, p_im + q_re], axis=1).astype(BF)
        lower = jnp.dot(s.turn[0], minus, preferred_element_type=F32)
        upper = jnp.dot(s.turn[1], plus, preferred_element_type=F32)
        row = lax.broadcasted_iota(jnp.int32, upper.shape, 0)
        upper = jnp.where(row == 0, zero_line, upper)
        for i in range(2):
            at = slice(i * LANES, i * LANES + cols)
            s.out[pair, i, :top] = (lower[:, at] * s.ncell[:top]).astype(BF)
            s.out[pair, i, top:] = (upper[:, at] * s.ncell[top:]).astype(BF)
        copy = pltpu.make_async_copy(s.out.at[pair], out_ref.at[pair], s.out_sem.at[pair])
        copy.start()
        return copy

    full = expanded(mask_ref[...].astype(F32))
    for t in range(full.shape[0]):
        s.mask[t] = full[t : t + 1]
    s.edge[...] = jnp.zeros_like(s.edge)
    fold(0)
    arrived()
    bins = bins_out()
    load(*((1, t) for t in range(tiles)), "rows", "cols")
    loaded("fy0", "cs")
    own, data = [columns(0, 0)], []
    loaded("fy1")
    own.append(columns(0, 1))
    own_edges = edges_out(0)
    own[0] = cells_to_chips(0, 0, own[0])
    fold(1)
    load("ty", "ft", "fx", "ts", "pick", "turn")
    data.append(columns(1, 0))
    own[1] = cells_to_chips(0, 1, own[1])
    bins = bins_on(bins)
    data.append(columns(1, 1))
    data_edges = edges_out(1)
    loaded("rows", "cols")
    own[0] = cells_done(0, 0, own[0])
    finish(bins)
    filter_cells()
    edges_done(0, own_edges)
    edges = partner_edges_out()
    own[1] = cells_done(0, 1, own[1])
    partner = [partner_out(0)]
    data[0] = cells_to_chips(1, 0, data[0])
    filters(0)
    partner.append(partner_out(1))
    data[1] = cells_to_chips(1, 1, data[1])
    filters(1)
    edges_done(1, data_edges)
    own[0] = gather_on(0, 0, own[0])
    loaded("ty", "ft")
    finish(own[0])
    make_y(0, 0, 0)
    own[1] = gather_on(0, 1, own[1])
    data[0] = cells_done(1, 0, data[0])
    legs_done(0, 0)
    data[1] = cells_done(1, 1, data[1])
    finish(own[1])
    make_y(0, 1, 0)
    data[0] = gather_on(1, 0, data[0])
    legs_done(0, 1)
    data[1] = gather_on(1, 1, data[1])
    finish(data[0])
    make_y(1, 0, 1)
    legs_done(1, 0)
    partner[0] = partner_on(0, partner[0])
    partner_edges(edges)
    finish(data[1])
    make_y(1, 1, 1)
    legs_done(1, 1)
    partner[1] = partner_on(1, partner[1])
    products()
    partner[0] = gather_on(2, 0, partner[0])
    loaded("fx", "ts", "pick", "turn")
    pair_cells(0)
    pair_sums(0)
    ds = [to_mate(0)]
    partner[1] = gather_on(2, 1, partner[1])
    pair_cells(1)
    ds[0] = first_out(0, ds[0])
    pair_sums(1)
    ds.append(to_mate(1))
    finish(partner[0])
    make_y(2, 0, 1)
    legs_done(1, 0)
    ds[1] = first_out(1, ds[1])
    finish(partner[1])
    make_y(2, 1, 1)
    ds[0] = second_out(0, ds[0])
    legs_done(1, 1)
    products()
    ds[1] = second_out(1, ds[1])
    pair_cells(2)
    pair_sums(2)
    ss = [to_mate(2)]
    pair_cells(3)
    pair_sums(3)
    ss.append(to_mate(3))
    ss[0] = first_out(2, ss[0])
    ds = each(last_out, 0, ds)
    ss[1] = first_out(3, ss[1])
    ds = assemble(0, ds)
    ss[0] = second_out(2, ss[0])
    ss[1] = second_out(3, ss[1])
    ss = each(last_out, 1, ss)
    assemble(1, ss).wait()
    ds.wait()


def estimates(sims, data, mask_flags, bins, signal, noise, norm, matching, nrows, nreal, nfield):
    h, npix = sims.shape
    kf, cols = bins.shape
    top, half = kf // 2, npix // 2
    t = constants(npix, kf, nrows)
    rows, pick_cols = cell_tables(kf)
    pick, turn = output_tables(kf, nrows)
    far, fields = max(nrows // 2 - 1, 1), max(nfield - 1, 1)
    chips = nrows // 2
    share = top // chips
    piece, block = (share, top), (top + TAIL, top)
    a_block, b_block = (top // 2, top), (top // 2 + TAIL, top)
    buf = lambda *shape: pltpu.VMEM(shape, BF)
    wide = lambda *shape: pltpu.VMEM(shape, F32)
    dma = lambda *shape: pltpu.SemaphoreType.DMA(shape)
    scratch = dict(
        maps=buf(2, h, npix), fy=buf(2, half, top), cs=buf(kf + TAIL, h), rows=buf(kf + TAIL, kf),
        cols=buf(kf, kf), ty=buf(h, kf), ft=buf(2, top, half), fx=buf(2, half, top),
        ts=buf(kf + TAIL, 2 * h), pick=buf(kf, 2 * LANES), turn=buf(2, top, top),
        idx=pltpu.VMEM((kf + TAIL, kf), jnp.int32), by_row=buf(kf + TAIL, kf),
        mask=wide(h // TILE, 1, npix), bins=buf(nrows, kf, cols), tab=wide(8, LANES),
        tabs=wide(6, top, top), lines=wide(8, kf),
        even=buf(h, half), odd=buf(h, half), zero_b=buf(h, LANES), cells=buf(h, top),
        fpart=buf(2, 2, nrows, *piece), fmate=buf(2, 2, chips, *piece), fchip=buf(2, 2, chips, *piece),
        ffar=buf(2, 2, far, *piece), pq=buf(3, 2, nrows, *piece), zin=buf(2, nreal - 1, *piece),
        ybuf=buf(2, 2, 3, h, top), ycol=wide(2, h, LANES), zbuf=buf(3, kf, top),
        own_legs=buf(3, 2, h, half), other=buf(3, 2, h, half), prods=buf(2, 2, h, half),
        zero=wide(h, LANES), wbuf=buf(2, 2 * h, top), ncell=wide(kf, cols),
        part=buf(4, 2, *block), mate_in=buf(4, *block), chip=buf(4, *block),
        a_field=buf(4, fields, *a_block), b_far=buf(4, far, *b_block), mid=buf(4, *block),
        a_far=buf(4, far, *a_block), b_field=buf(4, fields, *b_block), fin=buf(4, 2, *block),
        out=buf(2, 2, kf, cols), out_sem=dma(2), load_sem=dma(11), map_sem=dma(2, h // TILE), sbf=dma(far), rbf=dma(far), sbm=dma(chips), rbm=dma(chips),
        sf1=dma(2, 2), rf1=dma(2, 2), sf2=dma(2, 2, far), rf2=dma(2, 2, far),
        sgf=dma(3, 2, far), rgf=dma(3, 2, far), sgm=dma(3, 2, chips), rgm=dma(3, 2, chips),
        edge=wide(3, TAIL, LANES), edge_out=buf(2, TAIL, LANES), edge_in=buf(2, nrows - 1, TAIL, LANES),
        edge_z=buf(TAIL, LANES), edge_zin=buf(nreal - 1, TAIL, LANES),
        se=dma(2, nrows - 1), re=dma(2, nrows - 1), sez=dma(nreal - 1), rez=dma(nreal - 1),
        sz=dma(2, nreal - 1), rz=dma(2, nreal - 1),
        s1=dma(4), r1=dma(4), saf=dma(4, fields), raf=dma(4, fields),
        sbfield=dma(4, fields), rbfield=dma(4, fields),
        say=dma(4, far), ray=dma(4, far), sby=dma(4, far), rby=dma(4, far), s3=dma(4), r3=dma(4),
    )
    hbm = pl.BlockSpec(memory_space=pl.ANY)
    vmem = pl.BlockSpec(memory_space=pltpu.VMEM)
    smem = pl.BlockSpec(memory_space=pltpu.SMEM)
    tables = [t["fy"], t["cs"], rows, pick_cols, t["ty"], t["ft"], t["fx"], t["ts"], pick, turn]
    return pl.pallas_call(
        functools.partial(kernel, (nrows, nreal, nfield, t["unit"], t["step"]), tuple(scratch)),
        out_shape=jax.ShapeDtypeStruct((2, 2, kf, cols), BF),
        in_specs=[hbm] * 2 + [vmem] * 5 + [smem] + [hbm] * len(tables),
        out_specs=hbm,
        scratch_shapes=list(scratch.values()),
        compiler_params=pltpu.CompilerParams(
            collective_id=0, has_side_effects=True, vmem_limit_bytes=VMEM_LIMIT
        ),
        cost_estimate=pl.CostEstimate(
            flops=32 * h * npix * kf, bytes_accessed=24 * 2**20, transcendentals=0
        ),
    )(sims, data, mask_flags, bins, signal, noise, norm, matching, *(jnp.asarray(v) for v in tables))


def body(nrows, nreal, nfield, sims, data, mask_flags, bins, cl_signal, cl_noise, norm, matching):
    out = estimates(
        sims[0, 0], data[0], mask_flags, bins, cl_signal, cl_noise, norm[None], matching,
        nrows, nreal, nfield,
    )
    return out.astype(F32)[None]


def solution(mesh):
    in_specs = (
        P("real", "field", "rows", None),
        P("field", "rows", None),
        P("rows", None),
        P(None, "rows"),
        P("field", None),
        P("field", None),
        P(),
        P(),
    )
    out_specs = P("real", None, None, None, "rows")
    f = functools.partial(body, mesh.shape["rows"], mesh.shape["real"], mesh.shape["field"])
    return jax.shard_map(f, mesh=mesh, in_specs=in_specs, out_specs=out_specs, check_vma=False)
```
